32 devices in a mesh: shots: 2 (over y), depth: 2 (over core), lat: 8 (over z, x).
Axes of the slice: x: 2, y: 2, z: 4, core: 2. Of those that a mesh axis runs over, the one named last changes fastest.
Arguments:
- surface: float32 [4, 2, 1024, 1024], P('shots', None, 'lat'), parts along dimension 0, may hold values from -6 to 6
- slowness: float32 [2, 1024, 1024], P('depth', 'lat'), may hold values from 1.6 to 3.2
- stencil_coef: float32 [3, 2, 1024, 1024], P(None, 'depth', 'lat'), may hold values from 0.02 to 0.06
- base_slowness: float32 [8], replicated, may hold values from 2 to 2.8
- base_index: int32 [2], P('depth'), may hold values from 0 to 7
- frequency_table: float32 [16], replicated, may hold values from 0.6 to 1.2
- slot_frequency: int32 [4], P('shots'), parts along dimension 0, may hold values from 0 to 15
Outputs:
- migrated: float32 [4, 1024, 1024], P(('shots', 'depth'), 'lat'), parts along dimension 0
The draws below stay inside these ranges and needn't reach their ends.
There are 2 independent parts, one for each index of `shots`. The reference program is written for one: setup_inputs(seed, part) draws one part's arguments, and reference() takes and returns one part's arrays. A program takes and returns all parts, laid end to end along the dimension named above; an argument that names none is the same for every part. Nothing has to cross between parts.
All inputs are finite; a program needn't handle non-finite values.
Results may differ from the reference program's by a relative error of at most 0.0003.
Values sent between devices are 32-bit elements; how exact they have to be, the bound alone decides.
A program may use at most 64 MiB of HBM per device.

```python
import math
import jax
import jax.numpy as jnp
from jax import lax

NX = 1024
NY = 1024
SLOTS = 2
CORR = 3
NREF = 8
NFREQ = 16
NZ = 2


def block_levels(own_key, extent, shards, low, high):
    factor_of, own = 1.0, jax.random.fold_in(own_key, 6)
    for axis_at, shards_of in shards:
        heights = jnp.exp(jax.random.uniform(jax.random.fold_in(own, axis_at), (shards_of,), jnp.float32, low / len(shards), high / len(shards)))
        factor_of = factor_of * jnp.repeat(heights, extent[axis_at] // shards_of).reshape([-1 if axis == axis_at else 1 for axis in range(len(extent))])
    return factor_of


def centred(rng, shape, scale, limit, split=(), held_as=jnp.bfloat16):
    level = block_levels(rng, shape, split, -0.22, 0.18) if split else 1.0
    entries = jax.random.normal(rng, shape, jnp.float32) * scale * level
    return jnp.minimum(jnp.maximum(entries, -limit), limit).astype(held_as)


def setup_inputs(seed: int = 0, part: int = 0) -> dict:
    keys = jax.random.split(jax.random.key(seed), 8)
    part_splits = jax.random.split(jax.random.fold_in(keys[7], part), 8)
    surface = centred(part_splits[0], (SLOTS, 2, NX, NY), 1.0, 6.0, ((2, 8),), jnp.float32)
    slowness = jnp.clip(1.6 + 1.6 * jax.random.uniform(keys[1], (NZ, NX, NY), jnp.float32) ** block_levels(keys[1], (NZ, NX, NY), ((0, 2), (1, 8)), -0.2, 0.2), 1.6, 3.2)
    stencil_coef = jnp.clip(jnp.exp(math.log(0.06) - 1.0986123 * jax.random.uniform(keys[2], (CORR, NZ, NX, NY), jnp.float32) ** block_levels(keys[2], (CORR, NZ, NX, NY), ((1, 2), (2, 8)), -0.2, 0.2)), 0.02, 0.06)
    base_slowness = jnp.clip(jnp.exp(jax.random.uniform(keys[3], (NREF,), jnp.float32, math.log(2.0), math.log(2.8))), 2.0, 2.8)
    base_index = jax.random.randint(keys[4], (NZ,), 0, NREF).astype(jnp.int32)
    frequency_table = jnp.clip(jnp.exp(jax.random.uniform(keys[5], (NFREQ,), jnp.float32, math.log(0.6), math.log(1.2))), 0.6, 1.2)
    slot_frequency = jax.random.randint(part_splits[6], (SLOTS,), 0, NFREQ).astype(jnp.int32)
    return {"surface": surface, "slowness": slowness, "stencil_coef": stencil_coef, "base_slowness": base_slowness, "base_index": base_index, "frequency_table": frequency_table, "slot_frequency": slot_frequency}


depth_spacing = 1.0

def wavenumbers(count):
    index = jnp.arange(count, dtype=jnp.int32)
    signed = jnp.where(index < count // 2, index, index - count)
    return 2.0 * math.pi / count * signed.astype(jnp.float32)

def laplace(wavefield):
    padded = jnp.pad(wavefield, ((0, 0), (1, 1), (1, 1)))
    return padded[:, 2:, 1:-1] + padded[:, :-2, 1:-1] + padded[:, 1:-1, 2:] + padded[:, 1:-1, :-2] - 4.0 * wavefield

def reference(surface, slowness, stencil_coef, base_slowness, base_index, frequency_table, slot_frequency):
    omegas = frequency_table[slot_frequency]
    wavefield = lax.complex(surface[:, 0], surface[:, 1])
    wave_x = wavenumbers(NX)[:, None]
    wave_y = wavenumbers(NY)[None, :]
    lateral = wave_x ** 2 + wave_y ** 2
    layers = []
    for level in range(NZ):
        base_value = base_slowness[base_index[level]]
        spectrum = jnp.fft.fft2(wavefield, axes=(1, 2))
        vertical = ((omegas * base_value) ** 2)[:, None, None] - lateral[None]
        root = jnp.sqrt(jnp.abs(vertical))
        shifter = jnp.where(vertical > 0, jnp.exp(1j * depth_spacing * root), jnp.exp(-depth_spacing * root))
        wavefield = jnp.fft.ifft2(spectrum * shifter, axes=(1, 2))
        screen = depth_spacing * omegas[:, None, None] * (slowness[level] - base_value)[None]
        wavefield = wavefield * jnp.exp(1j * screen)
        for stencil in range(CORR):
            wavefield = wavefield + 1j * stencil_coef[stencil, level][None] * laplace(wavefield)
        layers.append(lax.optimization_barrier(jnp.sum(jnp.real(wavefield), axis=0)))
    return jnp.stack(layers)
```

```python
import math

import jax
import jax.numpy as jnp
from jax import lax
from jax.experimental import pallas as pl
from jax.experimental.pallas import tpu as pltpu
from jax.sharding import PartitionSpec as P

depth_spacing = 1.0
highest = lax.Precision.HIGHEST


def with_halo(cells, sides, width):
    for axis, dim in sides:
        count = lax.axis_size(axis)
        ends = count - 1
        head = lax.slice_in_dim(cells, 0, width, axis=dim)
        tail = lax.slice_in_dim(cells, cells.shape[dim] - width, cells.shape[dim], axis=dim)
        cells = jnp.concatenate(
            [
                lax.ppermute(tail, axis, [(i, (i + 1) % count) for i in range(ends)]),
                cells,
                lax.ppermute(head, axis, [((i + 1) % count, i) for i in range(ends)]),
            ],
            axis=dim,
        )
    return cells


def dft_table(count):
    row_index = lax.broadcasted_iota(jnp.int32, (count, count), 0)
    col_index = lax.broadcasted_iota(jnp.int32, (count, count), 1)
    angle = 2.0 * math.pi / count * (row_index * col_index % count).astype(jnp.float32)
    return (jnp.cos(angle), jnp.sin(angle))


def wavenumbers(index, count):
    signed = jnp.where(index < count // 2, index, index - count)
    return 2.0 * math.pi / count * signed.astype(jnp.float32)


def along_last(values, table):
    return jnp.einsum("brn,nk->brk", values, table, precision=highest)


def along_middle(values, table):
    return jnp.einsum("bxk,xj->bkj", values, table, precision=highest)


def pair_last(pair, table):
    batch = pair.shape[0]
    merged = pair.reshape((batch * 2,) + pair.shape[2:])
    result = along_last(merged, table)
    return result.reshape((batch, 2) + result.shape[1:])


def pair_middle(pair, table):
    batch = pair.shape[0]
    merged = pair.reshape((batch * 2,) + pair.shape[2:])
    result = along_middle(merged, table)
    return result.reshape((batch, 2) + result.shape[1:])


def stencil_sum(extended):
    center = extended[:, :, 1:-1]
    sideways = jnp.pad(center, ((0, 0), (0, 0), (0, 0), (1, 1)))
    return (
        extended[:, :, 2:]
        + extended[:, :, :-2]
        + sideways[..., 2:]
        + sideways[..., :-2]
        - 4.0 * center
    )


def correct(wavefield, stencil_value, coefficient):
    real_part = wavefield[:, 0] - coefficient[None] * stencil_value[:, 1]
    imag_part = wavefield[:, 1] + coefficient[None] * stencil_value[:, 0]
    return jnp.stack((real_part, imag_part), axis=1)


def shards(
    surface, slowness, stencil_coef, base_slowness, base_index, frequency_table, slot_frequency
):
    section_index = lax.axis_index("depth")
    sections = lax.axis_size("depth")
    lanes = lax.axis_size("lat")
    slots = surface.shape[0]
    rows = surface.shape[2]
    width_y = surface.shape[3]
    width_x = rows * lanes
    block_y = width_y // lanes
    steps_here = slowness.shape[0]
    stencils = stencil_coef.shape[0]
    cos_x, sin_x = dft_table(width_x)
    cos_y, sin_y = dft_table(width_y)
    wave_x = wavenumbers(lax.broadcasted_iota(jnp.int32, (width_x,), 0), width_x)[None, None, :]
    local_y = lax.axis_index("lat") * block_y + lax.broadcasted_iota(jnp.int32, (block_y,), 0)
    wave_y = wavenumbers(local_y, width_y)[None, :, None]
    lateral = wave_x**2 + wave_y**2
    table_freq = lax.broadcasted_iota(jnp.int32, (1, frequency_table.shape[0]), 1)
    omegas = jnp.sum(
        jnp.where(slot_frequency[:, None] == table_freq, frequency_table[None, :], 0.0), axis=1
    )
    table_base = lax.broadcasted_iota(jnp.int32, (1, base_slowness.shape[0]), 1)
    base_values = jnp.sum(
        jnp.where(base_index[:, None] == table_base, base_slowness[None, :], 0.0), axis=1
    )
    volume_slow, volume_coef, volume_base = (
        lax.all_gather(slowness, "depth", axis=0, tiled=True),
        lax.all_gather(stencil_coef, "depth", axis=1, tiled=True),
        lax.all_gather(base_values, "depth", axis=0, tiled=True),
    )
    levels = steps_here * sections
    mine = slots // sections
    first_mine = section_index * mine
    wavefield = lax.dynamic_slice_in_dim(surface, first_mine, mine, 0)
    freqs = lax.dynamic_slice_in_dim(omegas, first_mine, mine, 0)
    partial_layers = []
    for level in range(levels):
        depth_wavefield = wavefield
        batch = depth_wavefield.shape[0]
        base_value = volume_base[level]
        with_cos = pair_last(depth_wavefield, cos_y)
        with_sin = pair_last(depth_wavefield, sin_y)
        fwd_real = with_cos[:, 0] + with_sin[:, 1]
        fwd_imag = with_cos[:, 1] - with_sin[:, 0]
        packed = jnp.stack((fwd_real, fwd_imag), axis=1).reshape(batch, 2, rows, lanes, block_y)
        columns = lax.all_to_all(packed, "lat", split_axis=3, concat_axis=2, tiled=True).reshape(
            batch, 2, width_x, block_y
        )
        col_cos = pair_middle(columns, cos_x)
        col_sin = pair_middle(columns, sin_x)
        spec_real = col_cos[:, 0] + col_sin[:, 1]
        spec_imag = col_cos[:, 1] - col_sin[:, 0]
        vertical = ((freqs * base_value) ** 2)[:, None, None] - lateral
        root = jnp.sqrt(jnp.abs(vertical))
        shift_real = jnp.where(
            vertical > 0, jnp.cos(depth_spacing * root), jnp.exp(-depth_spacing * root)
        )
        shift_imag = jnp.where(vertical > 0, jnp.sin(depth_spacing * root), 0.0)
        moved = jnp.stack(
            (
                spec_real * shift_real - spec_imag * shift_imag,
                spec_real * shift_imag + spec_imag * shift_real,
            ),
            axis=1,
        )
        back_cos = pair_last(moved, cos_x)
        back_sin = pair_last(moved, sin_x)
        back_real = back_cos[:, 0] - back_sin[:, 1]
        back_imag = back_cos[:, 1] + back_sin[:, 0]
        packed = jnp.stack((back_real, back_imag), axis=1).reshape(batch, 2, block_y, lanes, rows)
        returned = lax.all_to_all(packed, "lat", split_axis=3, concat_axis=2, tiled=True).reshape(
            batch, 2, width_y, rows
        )
        scale = 1.0 / (width_x * width_y)
        ret_cos = pair_middle(returned, cos_y)
        ret_sin = pair_middle(returned, sin_y)
        out_real = (ret_cos[:, 0] - ret_sin[:, 1]) * scale
        out_imag = (ret_cos[:, 1] + ret_sin[:, 0]) * scale
        screen = depth_spacing * freqs[:, None, None] * (volume_slow[level] - base_value)[None]
        cosine = jnp.cos(screen)
        sine = jnp.sin(screen)
        depth_wavefield = jnp.stack(
            (out_real * cosine - out_imag * sine, out_real * sine + out_imag * cosine), axis=1
        )
        for stencil in range(stencils):
            extended = with_halo(depth_wavefield, (("lat", 2),), 1)
            depth_wavefield = correct(
                depth_wavefield, stencil_sum(extended), volume_coef[stencil, level]
            )
        wavefield = depth_wavefield
        partial_layers.append(jnp.sum(wavefield[:, 0], axis=0))
    partial_image = jnp.stack(partial_layers)
    return lax.psum_scatter(partial_image, "depth", scatter_dimension=0, tiled=True)


MESH = pl.DeviceIdType.MESH
tile_rows = 8
tile_lanes = 128
chunk = 16
gate_step = 1


def times_root(value, power, count, sign):
    real, imag = value
    turn = (power * 8 // count) % 8 if (power * 8) % count == 0 else None
    half = math.sqrt(0.5)
    if turn == 0:
        return value
    if turn == 2:
        return (-imag, real) if sign > 0 else (imag, -real)
    if turn == 1:
        if sign > 0:
            return ((real - imag) * half, (real + imag) * half)
        return ((real + imag) * half, (imag - real) * half)
    if turn == 3:
        if sign > 0:
            return (-(real + imag) * half, (real - imag) * half)
        return ((imag - real) * half, -(real + imag) * half)
    angle = sign * 2.0 * math.pi * power / count
    cosine, sine = math.cos(angle), math.sin(angle)
    return (real * cosine - imag * sine, real * sine + imag * cosine)


def short_dft(values, sign):
    count = len(values)
    if count == 1:
        return values
    even = short_dft(values[0::2], sign)
    odd = short_dft(values[1::2], sign)
    low, high = [], []
    for power in range(count // 2):
        turned = times_root(odd[power], power, count, sign)
        low.append((even[power][0] + turned[0], even[power][1] + turned[1]))
        high.append((even[power][0] - turned[0], even[power][1] - turned[1]))
    return low + high


def quarter_sincos(rest, quarter):
    square = rest * rest
    sine = rest + rest * square * (
        -1.6666654611e-1 + square * (8.3321608736e-3 + square * -1.9515295891e-4)
    )
    cosine = (
        1.0
        - 0.5 * square
        + square
        * square
        * (4.166664568298827e-2 + square * (-1.388731625493765e-3 + square * 2.443315711809948e-5))
    )
    swap = quarter % 2 == 1
    first = jnp.where(swap, cosine, sine)
    second = jnp.where(swap, sine, cosine)
    turn = quarter % 4
    return (
        jnp.where(turn >= 2, -first, first),
        jnp.where((turn == 1) | (turn == 2), -second, second),
    )


def sincos(angle):
    nearest = jnp.floor(angle * (2.0 / math.pi) + 0.5)
    rest = angle - nearest * 1.5703125
    rest = rest - nearest * 4.83751296997e-4
    rest = rest - nearest * 7.54978995489e-8
    return quarter_sincos(rest, nearest.astype(jnp.int32) & 3)


def split(values):
    high = values.astype(jnp.bfloat16)
    return high, (values - high.astype(jnp.float32)).astype(jnp.bfloat16)


def mul(left, right):
    return jnp.dot(left, right, preferred_element_type=jnp.float32)


def migrate_kernel(
    surface,
    slowness,
    coef,
    base_table,
    base_index,
    freq_table,
    slot_freq,
    out,
    field,
    fwd_hi,
    fwd_lo,
    bwd_hi,
    bwd_lo,
    short,
    after,
    phase,
    sent,
    got,
    back,
    ret,
    wide,
    coefs,
    slow,
    parcel,
    parcel_in,
    base,
    image,
    image_in,
    load_sem,
    vol_send,
    vol_recv,
    base_sem,
    send_sem,
    recv_sem,
    image_sem,
    turn,
    screen,
):
    lanes, rows2, width = short.shape
    rows = rows2 // 2
    ext = coefs.shape[2]
    halo = (ext - rows) // 2
    count = lanes * rows
    levels = coefs.shape[0]
    wire = rows + tile_rows
    half = lanes // 2
    far = lax.rem(lax.div(lax.axis_index("lat"), half) + 1, 2) * half
    near = lax.div(lax.axis_index("lat"), half) * half
    stencils = coef.shape[0]
    top = tile_rows
    own = top + halo
    me = lax.axis_index("lat")
    core = lax.axis_index("depth")
    other = 1 - core
    up = lax.rem(me + lanes - 1, lanes)
    down = lax.rem(me + 1, lanes)

    barrier = pltpu.get_barrier_semaphore()
    for step in range(1, lanes):
        pl.semaphore_signal(
            barrier,
            inc=1,
            device_id={"lat": lax.rem(me + step, lanes)},
            device_id_type=MESH,
        )
    for place in (me, up, down):
        pl.semaphore_signal(
            barrier, inc=1, device_id={"depth": other, "lat": place}, device_id_type=MESH
        )

    load = pltpu.make_async_copy(
        surface.at[core], field.at[0, :, pl.ds(own, rows), :], load_sem.at[0]
    )
    load.start()
    mine = [
        pltpu.make_async_copy(
            slowness.at[0], slow.at[core, pl.ds(0, rows), :], load_sem.at[1]
        ),
        pltpu.make_async_copy(
            coef.at[:, 0], coefs.at[core, :, pl.ds(halo, rows), :], load_sem.at[2]
        ),
    ]
    for copy in mine:
        copy.start()

    omega = freq_table[slot_freq[core]]
    base[core] = jnp.full(base.shape[1:], base_table[base_index[0]], jnp.float32)
    wide_y = field.shape[3]
    back[:, :, :, rows:, :] = jnp.zeros((levels, lanes, 2, tile_rows, width), jnp.float32)
    ret[:, :, :, rows:, :] = jnp.zeros((levels, lanes, 2, chunk, width), jnp.float32)
    slow[:, rows:, :] = jnp.zeros((levels, chunk, wide_y), jnp.float32)
    parcel[...] = jnp.zeros(parcel.shape, jnp.float32)
    rim = jnp.zeros((levels, stencils, halo, wide_y), jnp.float32)
    coefs[:, :, 0:halo, :] = rim
    coefs[:, :, halo + rows :, :] = rim
    edge = jnp.zeros((2, 2, top + halo, wide_y), jnp.float32)
    field[:, :, 0:own, :] = edge
    field[:, :, own + rows :, :] = edge

    def table(index, hi, lo, flip):
        def strip(at, carry):
            start = pl.multiple_of(at * chunk, chunk)
            row = start + lax.broadcasted_iota(jnp.int32, (chunk, width), 0)
            col = lax.broadcasted_iota(jnp.int32, (chunk, width), 1)
            power = col * (row * lanes + index) if flip else row * (col * lanes + index)
            power = power & (count - 1)
            quarter = (4 * power + count // 2) // count
            rest = power - quarter * (count // 4)
            sine, cosine = quarter_sincos(
                rest.astype(jnp.float32) * (2.0 * math.pi / count), quarter & 3
            )
            c_hi, c_lo = split(cosine)
            s_hi, s_lo = split(sine)
            n_hi, n_lo = -s_hi, -s_lo
            if flip:
                quads = ((c_hi, s_hi, n_hi, c_hi), (c_lo, s_lo, n_lo, c_lo))
            else:
                quads = ((c_hi, n_hi, s_hi, c_hi), (c_lo, n_lo, s_lo, c_lo))
            for ref, (aa, ab, ba, bb) in zip((hi, lo), quads):
                ref[index, pl.ds(start, chunk), 0:width] = aa
                ref[index, pl.ds(start, chunk), width:] = ab
                ref[index, pl.ds(rows + start, chunk), 0:width] = ba
                ref[index, pl.ds(rows + start, chunk), width:] = bb
            return carry

        lax.fori_loop(0, rows // chunk, strip, 0)

    def tables(hi, lo, flip):
        def body(index, carry):
            table(index, hi, lo, flip)
            return carry

        lax.fori_loop(0, lanes, body, 0)

    load.wait()

    def remote(src, dst, send, recv, device):
        return pltpu.make_async_remote_copy(
            src_ref=src,
            dst_ref=dst,
            send_sem=send,
            recv_sem=recv,
            device_id=device,
            device_id_type=MESH,
        )

    def volume_copies():
        whole = {"depth": other}
        found = [
            remote(base.at[core], base.at[core], base_sem.at[0], base_sem.at[1], whole),
            remote(
                slowness.at[0],
                slow.at[core, pl.ds(0, rows), :],
                vol_send.at[0],
                vol_recv.at[0],
                whole,
            ),
            remote(
                coef.at[:, 0],
                coefs.at[core, :, pl.ds(halo, rows), :],
                vol_send.at[1],
                vol_recv.at[1],
                whole,
            ),
        ]
        targets = ((core, up, 0), (other, up, 0), (core, down, 1), (other, down, 1))
        for at, (section, place, side) in enumerate(targets):
            found.append(
                remote(
                    parcel.at[side],
                    parcel_in.at[core, side],
                    vol_send.at[2 + at],
                    vol_recv.at[2 + at],
                    {"depth": section, "lat": place},
                )
            )
        return found

    def parcel_rows():
        at = 0
        for stencil in range(stencils - 1):
            size = stencils - 1 - stencil
            yield stencil, at, size
            at += size
        yield stencils, at, stencils

    def pack_parcels():
        for which, at, size in parcel_rows():
            if which < stencils:
                first = coefs[core, which, halo : halo + size, :]
                last = coefs[core, which, halo + rows - size : halo + rows, :]
            else:
                first = slow[core, 0:size, :]
                last = slow[core, rows - size : rows, :]
            parcel[0, at : at + size, :] = first
            parcel[1, at : at + size, :] = last

    def unpack_parcels():
        for level in range(levels):
            for which, at, size in parcel_rows():
                below = parcel_in[level, 0, at : at + size, :]
                above = parcel_in[level, 1, at : at + size, :]
                if which < stencils:
                    coefs[level, which, halo - size : halo, :] = above * inside_first
                    coefs[level, which, halo + rows : halo + rows + size, :] = (
                        below * inside_last
                    )
                else:
                    slow[level, rows : rows + size, :] = above
                    slow[level, rows + size : rows + 2 * size, :] = below

    inside_first = jnp.where(me > 0, 1.0, 0.0)
    inside_last = jnp.where(me < lanes - 1, 1.0, 0.0)

    def wavenumber(index):
        signed = jnp.where(index < count // 2, index, index - count)
        return 2.0 * math.pi / count * signed.astype(jnp.float32)

    def make_phase(level):
        edge_q = (omega * base[level][0:1, :]) ** 2

        def body(index, carry):
            def strip(at, inner):
                start = pl.multiple_of(at * chunk, chunk)
                row = start + lax.broadcasted_iota(jnp.int32, (chunk, width), 0)
                col = lax.broadcasted_iota(jnp.int32, (chunk, width), 1)
                lateral = (
                    wavenumber(row * lanes + index) ** 2 + wavenumber(col * lanes + me) ** 2
                )
                vertical = edge_q - lateral
                root = jnp.sqrt(jnp.abs(vertical))
                sine, cosine = sincos(depth_spacing * root)
                fade = jnp.exp(-depth_spacing * root)
                scale = 1.0 / (count * count)
                moving = vertical > 0
                phase[index, pl.ds(start, chunk), :] = jnp.where(moving, cosine, fade) * scale
                phase[index, pl.ds(rows + start, chunk), :] = (
                    jnp.where(moving, sine, 0.0) * scale
                )
                return inner

            lax.fori_loop(0, rows // chunk, strip, 0)
            return carry

        lax.fori_loop(0, lanes, body, 0)

    quarter = lax.div(me * 4, lanes)
    outer = 1 - lax.div(lax.rem(quarter + 1, 4), 2)

    def peer_at(step):
        place = lax.rem(step + outer * half, lanes - 1)
        beside = lax.div(place, half)
        return far + beside * (near - far) + lax.rem(me + place + beside, half)

    def each_peer(body, low=0, high=lanes - 1):
        def at(step, carry):
            body(peer_at(step))
            return carry

        lax.fori_loop(low, high, at, 0)

    gated = min(gate_step, lanes - 2)

    def take_turn(phase):
        @pl.when((core == 1) | (phase > 0))
        def _():
            pl.semaphore_wait(turn.at[2 * phase + core], 1)

    def pass_turn(phase, sent_to):
        def one(peer):
            sent_to(peer).wait_send()

        each_peer(one, 0, gated + 1)

        @pl.when((core == 0) | (phase < 2 * levels - 1))
        def _():
            pl.semaphore_signal(
                turn.at[2 * phase + core + 1],
                inc=1,
                device_id={"depth": other},
                device_id_type=MESH,
            )

    volume = volume_copies()
    swap = remote(
        image.at[other], image_in, image_sem.at[0], image_sem.at[1], {"depth": other}
    )
    for level in range(levels):
        source = 0 if level == 0 else stencils % 2

        def split_rows(at, carry):
            start = pl.multiple_of(at * chunk, chunk)
            values = [
                tuple(
                    field[source, part, pl.ds(own + start, chunk), a * width : (a + 1) * width]
                    for part in range(2)
                )
                for a in range(lanes)
            ]
            for d, (real, imag) in enumerate(short_dft(values, -1)):
                wide[d, pl.ds(start, chunk), 0:width] = real
                wide[d, pl.ds(start, chunk), width:] = imag
            return carry

        lax.fori_loop(0, rows // chunk, split_rows, 0)

        def forward(d):
            hi, lo = split(wide[d, 0:rows, :])
            made = mul(jnp.concatenate([hi, lo], axis=0), fwd_hi[d])
            return made[:rows] + made[rows:] + mul(hi, fwd_lo[d])

        if level == 0:
            pl.semaphore_wait(barrier, lanes + 2)

        def there(peer):
            return remote(
                sent.at[level, peer],
                got.at[level, me],
                send_sem.at[level, 0, peer],
                recv_sem.at[level, 0, me],
                {"lat": peer},
            )

        def send_forward(peer):
            if level == 0:
                table(peer, fwd_hi, fwd_lo, False)
            made = forward(peer)
            sent[level, peer, 0:rows, :] = made[:, 0:width]
            sent[level, peer, rows:, :] = made[:, width:]
            there(peer).start()

        def prepare():
            tables(bwd_hi, bwd_lo, True)
            volume[0].wait()
            make_phase(level)

        if level == 0:
            for copy in volume[:3]:
                copy.start()

            @pl.when(core == 1)
            def _():
                prepare()

        take_turn(2 * level)
        each_peer(send_forward)
        if level == 0:
            table(me, fwd_hi, fwd_lo, False)
        made = forward(me)
        got[level, me, 0:rows, :] = made[:, 0:width]
        got[level, me, rows:, :] = made[:, width:]

        if level == 0:
            for copy in mine:
                copy.wait()
            pack_parcels()
            for copy in volume[3:]:
                copy.start()

            @pl.when(core == 0)
            def _():
                prepare()

        else:
            make_phase(level)
        pass_turn(2 * level, there)

        def arrive_forward(peer):
            remote(
                sent.at[level, me],
                got.at[level, peer],
                send_sem.at[level, 0, me],
                recv_sem.at[level, 0, peer],
                {"lat": peer},
            ).wait_recv()

        each_peer(arrive_forward)

        def split_columns(at, carry):
            start = pl.multiple_of(at * chunk, chunk)
            values = [
                (
                    got[level, r, pl.ds(start, chunk), :],
                    got[level, r, pl.ds(rows + start, chunk), :],
                )
                for r in range(lanes)
            ]
            for e, (real, imag) in enumerate(short_dft(values, -1)):
                short[e, pl.ds(start, chunk), :] = real
                short[e, pl.ds(rows + start, chunk), :] = imag
            return carry

        lax.fori_loop(0, rows // chunk, split_columns, 0)

        def left(hi_table, lo_table, values):
            hi, lo = split(values)
            made = mul(hi_table, jnp.concatenate([hi, lo], axis=1))
            return made[:, 0:width] + made[:, width:] + mul(lo_table, hi)

        def column(e, carry):
            after[e] = left(bwd_hi[e], bwd_lo[e], short[e])
            return carry

        def shifted(e, carry):
            real, imag = after[e, 0:rows, :], after[e, rows:, :]
            shift_real, shift_imag = phase[e, 0:rows, :], phase[e, rows:, :]
            moved = jnp.concatenate(
                [
                    real * shift_real - imag * shift_imag,
                    real * shift_imag + imag * shift_real,
                ],
                axis=0,
            )
            after[e] = left(fwd_hi[e], fwd_lo[e], moved)
            return carry

        lax.fori_loop(0, lanes, column, 0, unroll=2)
        lax.fori_loop(0, lanes, shifted, 0, unroll=2)

        def join_columns(at, carry):
            start = pl.multiple_of(at * chunk, chunk)
            values = [
                (after[e, pl.ds(start, chunk), :], after[e, pl.ds(rows + start, chunk), :])
                for e in range(lanes)
            ]
            for r, (real, imag) in enumerate(short_dft(values, 1)):
                back[level, r, 0, pl.ds(start, chunk), :] = real
                back[level, r, 1, pl.ds(start, chunk), :] = imag
            return carry

        lax.fori_loop(0, rows // chunk, join_columns, 0)
        for r in range(lanes):
            for part in range(2):
                back[level, r, part, rows : rows + stencils, :] = back[
                    level, (r - 1) % lanes, part, rows - stencils : rows, :
                ]
                back[level, r, part, rows + stencils : rows + 2 * stencils, :] = back[
                    level, (r + 1) % lanes, part, 0:stencils, :
                ]

        def home(peer):
            return remote(
                back.at[level, peer],
                ret.at[level, me, :, pl.ds(0, wire), :],
                send_sem.at[level, 1, peer],
                recv_sem.at[level, 1, me],
                {"lat": peer},
            )

        take_turn(2 * level + 1)
        each_peer(lambda peer: home(peer).start())

        def inverse(d, real, imag):
            hi, lo = split(jnp.concatenate([real, imag], axis=1))
            wide[d] = mul(hi, bwd_hi[d]) + mul(lo, bwd_hi[d]) + mul(hi, bwd_lo[d])

        for part in range(2):
            ret[level, me, part, 0:wire, :] = back[level, me, part]
        inverse(me, ret[level, me, 0], ret[level, me, 1])
        pass_turn(2 * level + 1, home)

        if level == 0:
            for copy in volume[1:]:
                copy.wait()
            unpack_parcels()

        def make_screen(at, carry):
            start = pl.multiple_of(at * chunk, chunk)
            for a in range(lanes):
                cols = slice(a * width, (a + 1) * width)
                gap = slow[level, pl.ds(start, chunk), cols] - base[level][0:1, :]
                sine, cosine = sincos(depth_spacing * omega * gap)
                screen[0, pl.ds(start, chunk), cols] = cosine
                screen[1, pl.ds(start, chunk), cols] = sine
            return carry

        lax.fori_loop(0, rows // chunk + 1, make_screen, 0)

        def arrive_back(peer):
            remote(
                back.at[level, me],
                ret.at[level, peer, :, pl.ds(0, wire), :],
                send_sem.at[level, 1, me],
                recv_sem.at[level, 1, peer],
                {"lat": peer},
            ).wait_recv()
            inverse(peer, ret[level, peer, 0], ret[level, peer, 1])

        each_peer(arrive_back)

        def screened(start):
            values = [
                (wide[d, pl.ds(start, chunk), 0:width], wide[d, pl.ds(start, chunk), width:])
                for d in range(lanes)
            ]
            for a, (real, imag) in enumerate(short_dft(values, 1)):
                cols = slice(a * width, (a + 1) * width)
                cosine = screen[0, pl.ds(start, chunk), cols]
                sine = screen[1, pl.ds(start, chunk), cols]
                yield cols, (real * cosine - imag * sine, real * sine + imag * cosine)

        def join_rows(at, carry):
            start = pl.multiple_of(at * chunk, chunk)
            for cols, pair in screened(start):
                for part, value in enumerate(pair):
                    field[0, part, pl.ds(own + start, chunk), cols] = value
            return carry

        lax.fori_loop(0, rows // chunk, join_rows, 0)
        for cols, pair in screened(rows):
            for part, value in enumerate(pair):
                field[0, part, own - stencils : own, cols] = value[0:stencils] * inside_first
                field[0, part, own + rows : own + rows + stencils, cols] = (
                    value[stencils : 2 * stencils] * inside_last
                )

        lane = lax.broadcasted_iota(jnp.int32, (chunk, wide_y), 1)

        def neighbours(ref_at, part, start, center):
            left_one = jnp.where(lane == 0, 0.0, pltpu.roll(center, 1, axis=1))
            right_one = jnp.where(
                lane == wide_y - 1, 0.0, pltpu.roll(center, wide_y - 1, axis=1)
            )
            return (
                field[ref_at, part, start - 1 : start - 1 + chunk, :]
                + field[ref_at, part, start + 1 : start + 1 + chunk, :]
                + left_one
                + right_one
                - 4.0 * center
            )

        for stencil in range(stencils):
            now, later = stencil % 2, (stencil + 1) % 2
            final = stencil == stencils - 1
            for start in range(own if final else top, own + rows if final else top + ext, chunk):
                real = field[now, 0, start : start + chunk, :]
                imag = field[now, 1, start : start + chunk, :]
                weight = coefs[level, stencil, start - top : start - top + chunk, :]
                new_real = real - weight * neighbours(now, 1, start, imag)
                field[later, 0, start : start + chunk, :] = new_real
                if final:
                    image[level, start - own : start - own + chunk, :] = new_real
                field[later, 1, start : start + chunk, :] = imag + weight * neighbours(
                    now, 0, start, real
                )

        @pl.when(core != level)
        def _():
            swap.start()

    def drain(peer):
        for level in range(levels):
            for way, src, dst in (
                (0, sent.at[level, peer], got.at[level, me]),
                (1, back.at[level, peer], ret.at[level, me, :, pl.ds(0, wire), :]),
            ):
                remote(
                    src,
                    dst,
                    send_sem.at[level, way, peer],
                    recv_sem.at[level, way, me],
                    {"lat": peer},
                ).wait_send()

    each_peer(drain, gated + 1)
    swap.wait()
    out[0] = image[core] + image_in[...]


def fused(
    surface, slowness, stencil_coef, base_slowness, base_index, frequency_table, slot_frequency
):
    lanes = lax.axis_size("lat")
    sections = lax.axis_size("depth")
    rows, wide_y = surface.shape[2:]
    stencils = stencil_coef.shape[0]
    width = wide_y // lanes
    halo = -(-stencils // tile_rows) * tile_rows
    ext = rows + 2 * halo
    levels = sections
    parcel = -(-stencils * (stencils + 1) // (2 * tile_rows)) * tile_rows
    f32, bf16 = jnp.float32, jnp.bfloat16
    vmem, smem = pltpu.VMEM, pltpu.SMEM
    sem = pltpu.SemaphoreType.DMA
    anywhere = pl.BlockSpec(memory_space=pltpu.HBM)
    scalar = pl.BlockSpec(memory_space=smem)
    return pl.pallas_call(
        migrate_kernel,
        out_shape=vmem((1, rows, wide_y), f32),
        in_specs=[anywhere] * 3 + [scalar] * 4,
        out_specs=pl.BlockSpec(memory_space=vmem),
        scratch_shapes=[
            vmem((2, 2, ext + 2 * tile_rows, wide_y), f32),
            vmem((lanes, 2 * rows, 2 * width), bf16),
            vmem((lanes, 2 * rows, 2 * width), bf16),
            vmem((lanes, 2 * rows, 2 * width), bf16),
            vmem((lanes, 2 * rows, 2 * width), bf16),
            vmem((lanes, 2 * rows, width), f32),
            vmem((lanes, 2 * rows, width), f32),
            vmem((lanes, 2 * rows, width), f32),
            vmem((levels, lanes, 2 * rows, width), f32),
            vmem((levels, lanes, 2 * rows, width), f32),
            vmem((levels, lanes, 2, rows + tile_rows, width), f32),
            vmem((levels, lanes, 2, rows + chunk, width), f32),
            vmem((lanes, rows + chunk, 2 * width), f32),
            vmem((levels, stencils, ext, wide_y), f32),
            vmem((levels, rows + chunk, wide_y), f32),
            vmem((2, parcel, wide_y), f32),
            vmem((levels, 2, parcel, wide_y), f32),
            vmem((levels, tile_rows, tile_lanes), f32),
            vmem((levels, rows, wide_y), f32),
            vmem((rows, wide_y), f32),
            sem((3,)),
            sem((6,)),
            sem((6,)),
            sem((2,)),
            sem((levels, 2, lanes)),
            sem((levels, 2, lanes)),
            sem((2,)),
            pltpu.SemaphoreType.REGULAR((4 * levels,)),
            vmem((2, rows + chunk, wide_y), f32),
        ],
        compiler_params=pltpu.CompilerParams(
            collective_id=0, has_side_effects=True, vmem_limit_bytes=62 * 2**20
        ),
    )(surface, slowness, stencil_coef, base_slowness, base_index, frequency_table, slot_frequency)


def migrate(*arrays):
    surface, slowness, stencil_coef = arrays[:3]
    lanes = lax.axis_size("lat")
    sections = lax.axis_size("depth")
    rows, wide_y = surface.shape[2:]
    fits = (
        rows * lanes == wide_y
        and rows == tile_lanes
        and lanes > 1
        and lanes & (lanes - 1) == 0
        and sections == 2
        and surface.shape[0] == sections
        and slowness.shape[0] == 1
        and 0 < 2 * stencil_coef.shape[0] <= tile_rows
    )
    return fused(*arrays) if fits else shards(*arrays)


def solution(mesh):
    placed = (
        P("shots", None, "lat", None),
        P("depth", "lat", None),
        P(None, "depth", "lat", None),
        P(),
        P("depth"),
        P(),
        P("shots"),
    )
    return jax.shard_map(
        migrate,
        mesh=mesh,
        in_specs=placed,
        out_specs=P(("shots", "depth"), "lat", None),
        check_vma=False,
    )
```

```python
import math

import jax
import jax.numpy as jnp
from jax import lax
from jax.experimental import pallas as pl
from jax.experimental.pallas import tpu as pltpu
from jax.sharding import PartitionSpec as P

depth_spacing = 1.0
highest = lax.Precision.HIGHEST


def with_halo(cells, sides, width):
    for axis, dim in sides:
        count = lax.axis_size(axis)
        ends = count - 1
        head = lax.slice_in_dim(cells, 0, width, axis=dim)
        tail = lax.slice_in_dim(cells, cells.shape[dim] - width, cells.shape[dim], axis=dim)
        cells = jnp.concatenate(
            [
                lax.ppermute(tail, axis, [(i, (i + 1) % count) for i in range(ends)]),
                cells,
                lax.ppermute(head, axis, [((i + 1) % count, i) for i in range(ends)]),
            ],
            axis=dim,
        )
    return cells


def dft_table(count):
    row_index = lax.broadcasted_iota(jnp.int32, (count, count), 0)
    col_index = lax.broadcasted_iota(jnp.int32, (count, count), 1)
    angle = 2.0 * math.pi / count * (row_index * col_index % count).astype(jnp.float32)
    return (jnp.cos(angle), jnp.sin(angle))


def wavenumbers(index, count):
    signed = jnp.where(index < count // 2, index, index - count)
    return 2.0 * math.pi / count * signed.astype(jnp.float32)


def along_last(values, table):
    return jnp.einsum("brn,nk->brk", values, table, precision=highest)


def along_middle(values, table):
    return jnp.einsum("bxk,xj->bkj", values, table, precision=highest)


def pair_last(pair, table):
    batch = pair.shape[0]
    merged = pair.reshape((batch * 2,) + pair.shape[2:])
    result = along_last(merged, table)
    return result.reshape((batch, 2) + result.shape[1:])


def pair_middle(pair, table):
    batch = pair.shape[0]
    merged = pair.reshape((batch * 2,) + pair.shape[2:])
    result = along_middle(merged, table)
    return result.reshape((batch, 2) + result.shape[1:])


def stencil_sum(extended):
    center = extended[:, :, 1:-1]
    sideways = jnp.pad(center, ((0, 0), (0, 0), (0, 0), (1, 1)))
    return (
        extended[:, :, 2:]
        + extended[:, :, :-2]
        + sideways[..., 2:]
        + sideways[..., :-2]
        - 4.0 * center
    )


def correct(wavefield, stencil_value, coefficient):
    real_part = wavefield[:, 0] - coefficient[None] * stencil_value[:, 1]
    imag_part = wavefield[:, 1] + coefficient[None] * stencil_value[:, 0]
    return jnp.stack((real_part, imag_part), axis=1)


def shards(
    surface, slowness, stencil_coef, base_slowness, base_index, frequency_table, slot_frequency
):
    section_index = lax.axis_index("depth")
    sections = lax.axis_size("depth")
    lanes = lax.axis_size("lat")
    slots = surface.shape[0]
    rows = surface.shape[2]
    width_y = surface.shape[3]
    width_x = rows * lanes
    block_y = width_y // lanes
    steps_here = slowness.shape[0]
    stencils = stencil_coef.shape[0]
    cos_x, sin_x = dft_table(width_x)
    cos_y, sin_y = dft_table(width_y)
    wave_x = wavenumbers(lax.broadcasted_iota(jnp.int32, (width_x,), 0), width_x)[None, None, :]
    local_y = lax.axis_index("lat") * block_y + lax.broadcasted_iota(jnp.int32, (block_y,), 0)
    wave_y = wavenumbers(local_y, width_y)[None, :, None]
    lateral = wave_x**2 + wave_y**2
    table_freq = lax.broadcasted_iota(jnp.int32, (1, frequency_table.shape[0]), 1)
    omegas = jnp.sum(
        jnp.where(slot_frequency[:, None] == table_freq, frequency_table[None, :], 0.0), axis=1
    )
    table_base = lax.broadcasted_iota(jnp.int32, (1, base_slowness.shape[0]), 1)
    base_values = jnp.sum(
        jnp.where(base_index[:, None] == table_base, base_slowness[None, :], 0.0), axis=1
    )
    volume_slow, volume_coef, volume_base = (
        lax.all_gather(slowness, "depth", axis=0, tiled=True),
        lax.all_gather(stencil_coef, "depth", axis=1, tiled=True),
        lax.all_gather(base_values, "depth", axis=0, tiled=True),
    )
    levels = steps_here * sections
    mine = slots // sections
    first_mine = section_index * mine
    wavefield = lax.dynamic_slice_in_dim(surface, first_mine, mine, 0)
    freqs = lax.dynamic_slice_in_dim(omegas, first_mine, mine, 0)
    partial_layers = []
    for level in range(levels):
        depth_wavefield = wavefield
        batch = depth_wavefield.shape[0]
        base_value = volume_base[level]
        with_cos = pair_last(depth_wavefield, cos_y)
        with_sin = pair_last(depth_wavefield, sin_y)
        fwd_real = with_cos[:, 0] + with_sin[:, 1]
        fwd_imag = with_cos[:, 1] - with_sin[:, 0]
        packed = jnp.stack((fwd_real, fwd_imag), axis=1).reshape(batch, 2, rows, lanes, block_y)
        columns = lax.all_to_all(packed, "lat", split_axis=3, concat_axis=2, tiled=True).reshape(
            batch, 2, width_x, block_y
        )
        col_cos = pair_middle(columns, cos_x)
        col_sin = pair_middle(columns, sin_x)
        spec_real = col_cos[:, 0] + col_sin[:, 1]
        spec_imag = col_cos[:, 1] - col_sin[:, 0]
        vertical = ((freqs * base_value) ** 2)[:, None, None] - lateral
        root = jnp.sqrt(jnp.abs(vertical))
        shift_real = jnp.where(
            vertical > 0, jnp.cos(depth_spacing * root), jnp.exp(-depth_spacing * root)
        )
        shift_imag = jnp.where(vertical > 0, jnp.sin(depth_spacing * root), 0.0)
        moved = jnp.stack(
            (
                spec_real * shift_real - spec_imag * shift_imag,
                spec_real * shift_imag + spec_imag * shift_real,
            ),
            axis=1,
        )
        back_cos = pair_last(moved, cos_x)
        back_sin = pair_last(moved, sin_x)
        back_real = back_cos[:, 0] - back_sin[:, 1]
        back_imag = back_cos[:, 1] + back_sin[:, 0]
        packed = jnp.stack((back_real, back_imag), axis=1).reshape(batch, 2, block_y, lanes, rows)
        returned = lax.all_to_all(packed, "lat", split_axis=3, concat_axis=2, tiled=True).reshape(
            batch, 2, width_y, rows
        )
        scale = 1.0 / (width_x * width_y)
        ret_cos = pair_middle(returned, cos_y)
        ret_sin = pair_middle(returned, sin_y)
        out_real = (ret_cos[:, 0] - ret_sin[:, 1]) * scale
        out_imag = (ret_cos[:, 1] + ret_sin[:, 0]) * scale
        screen = depth_spacing * freqs[:, None, None] * (volume_slow[level] - base_value)[None]
        cosine = jnp.cos(screen)
        sine = jnp.sin(screen)
        depth_wavefield = jnp.stack(
            (out_real * cosine - out_imag * sine, out_real * sine + out_imag * cosine), axis=1
        )
        for stencil in range(stencils):
            extended = with_halo(depth_wavefield, (("lat", 2),), 1)
            depth_wavefield = correct(
                depth_wavefield, stencil_sum(extended), volume_coef[stencil, level]
            )
        wavefield = depth_wavefield
        partial_layers.append(jnp.sum(wavefield[:, 0], axis=0))
    partial_image = jnp.stack(partial_layers)
    return lax.psum_scatter(partial_image, "depth", scatter_dimension=0, tiled=True)


MESH = pl.DeviceIdType.MESH
tile_rows = 8
tile_lanes = 128
chunk = 16
gate_step = 2


def times_root(value, power, count, sign):
    real, imag = value
    turn = (power * 8 // count) % 8 if (power * 8) % count == 0 else None
    half = math.sqrt(0.5)
    if turn == 0:
        return value
    if turn == 2:
        return (-imag, real) if sign > 0 else (imag, -real)
    if turn == 1:
        if sign > 0:
            return ((real - imag) * half, (real + imag) * half)
        return ((real + imag) * half, (imag - real) * half)
    if turn == 3:
        if sign > 0:
            return (-(real + imag) * half, (real - imag) * half)
        return ((imag - real) * half, -(real + imag) * half)
    angle = sign * 2.0 * math.pi * power / count
    cosine, sine = math.cos(angle), math.sin(angle)
    return (real * cosine - imag * sine, real * sine + imag * cosine)


def short_dft(values, sign):
    count = len(values)
    if count == 1:
        return values
    even = short_dft(values[0::2], sign)
    odd = short_dft(values[1::2], sign)
    low, high = [], []
    for power in range(count // 2):
        turned = times_root(odd[power], power, count, sign)
        low.append((even[power][0] + turned[0], even[power][1] + turned[1]))
        high.append((even[power][0] - turned[0], even[power][1] - turned[1]))
    return low + high


def quarter_sincos(rest, quarter):
    square = rest * rest
    sine = rest + rest * square * (
        -1.6666654611e-1 + square * (8.3321608736e-3 + square * -1.9515295891e-4)
    )
    cosine = (
        1.0
        - 0.5 * square
        + square
        * square
        * (4.166664568298827e-2 + square * (-1.388731625493765e-3 + square * 2.443315711809948e-5))
    )
    swap = quarter % 2 == 1
    first = jnp.where(swap, cosine, sine)
    second = jnp.where(swap, sine, cosine)
    turn = quarter % 4
    return (
        jnp.where(turn >= 2, -first, first),
        jnp.where((turn == 1) | (turn == 2), -second, second),
    )


def sincos(angle):
    nearest = jnp.floor(angle * (2.0 / math.pi) + 0.5)
    rest = angle - nearest * 1.5703125
    rest = rest - nearest * 4.83751296997e-4
    rest = rest - nearest * 7.54978995489e-8
    return quarter_sincos(rest, nearest.astype(jnp.int32) & 3)


def split(values):
    high = values.astype(jnp.bfloat16)
    return high, (values - high.astype(jnp.float32)).astype(jnp.bfloat16)


def mul(left, right):
    return jnp.dot(left, right, preferred_element_type=jnp.float32)


def migrate_kernel(
    surface,
    slowness,
    coef,
    base_table,
    base_index,
    freq_table,
    slot_freq,
    out,
    field,
    fwd_hi,
    fwd_lo,
    bwd_hi,
    bwd_lo,
    short,
    after,
    phase,
    sent,
    got,
    back,
    ret,
    wide,
    coefs,
    slow,
    parcel,
    parcel_in,
    base,
    image,
    image_in,
    load_sem,
    vol_send,
    vol_recv,
    base_sem,
    send_sem,
    recv_sem,
    image_sem,
    turn,
    screen,
):
    lanes, rows2, width = short.shape
    rows = rows2 // 2
    ext = coefs.shape[2]
    halo = (ext - rows) // 2
    count = lanes * rows
    levels = coefs.shape[0]
    wire = rows + tile_rows
    half = lanes // 2
    far = lax.rem(lax.div(lax.axis_index("lat"), half) + 1, 2) * half
    near = lax.div(lax.axis_index("lat"), half) * half
    stencils = coef.shape[0]
    top = tile_rows
    own = top + halo
    me = lax.axis_index("lat")
    core = lax.axis_index("depth")
    other = 1 - core
    up = lax.rem(me + lanes - 1, lanes)
    down = lax.rem(me + 1, lanes)

    barrier = pltpu.get_barrier_semaphore()
    for step in range(1, lanes):
        pl.semaphore_signal(
            barrier,
            inc=1,
            device_id={"lat": lax.rem(me + step, lanes)},
            device_id_type=MESH,
        )
    for place in (me, up, down):
        pl.semaphore_signal(
            barrier, inc=1, device_id={"depth": other, "lat": place}, device_id_type=MESH
        )

    load = pltpu.make_async_copy(
        surface.at[core], field.at[0, :, pl.ds(own, rows), :], load_sem.at[0]
    )
    load.start()
    mine = [
        pltpu.make_async_copy(
            slowness.at[0], slow.at[core, pl.ds(0, rows), :], load_sem.at[1]
        ),
        pltpu.make_async_copy(
            coef.at[:, 0], coefs.at[core, :, pl.ds(halo, rows), :], load_sem.at[2]
        ),
    ]
    for copy in mine:
        copy.start()

    omega = freq_table[slot_freq[core]]
    base[core] = jnp.full(base.shape[1:], base_table[base_index[0]], jnp.float32)
    wide_y = field.shape[3]
    back[:, :, :, rows:, :] = jnp.zeros((levels, lanes, 2, tile_rows, width), jnp.float32)
    ret[:, :, :, rows:, :] = jnp.zeros((levels, lanes, 2, chunk, width), jnp.float32)
    slow[:, rows:, :] = jnp.zeros((levels, chunk, wide_y), jnp.float32)
    parcel[...] = jnp.zeros(parcel.shape, jnp.float32)
    rim = jnp.zeros((levels, stencils, halo, wide_y), jnp.float32)
    coefs[:, :, 0:halo, :] = rim
    coefs[:, :, halo + rows :, :] = rim
    edge = jnp.zeros((2, 2, top + halo, wide_y), jnp.float32)
    field[:, :, 0:own, :] = edge
    field[:, :, own + rows :, :] = edge

    def table(index, hi, lo, flip):
        def strip(at, carry):
            start = pl.multiple_of(at * chunk, chunk)
            row = start + lax.broadcasted_iota(jnp.int32, (chunk, width), 0)
            col = lax.broadcasted_iota(jnp.int32, (chunk, width), 1)
            power = col * (row * lanes + index) if flip else row * (col * lanes + index)
            power = power & (count - 1)
            quarter = (4 * power + count // 2) // count
            rest = power - quarter * (count // 4)
            sine, cosine = quarter_sincos(
                rest.astype(jnp.float32) * (2.0 * math.pi / count), quarter & 3
            )
            c_hi, c_lo = split(cosine)
            s_hi, s_lo = split(sine)
            n_hi, n_lo = -s_hi, -s_lo
            if flip:
                quads = ((c_hi, s_hi, n_hi, c_hi), (c_lo, s_lo, n_lo, c_lo))
            else:
                quads = ((c_hi, n_hi, s_hi, c_hi), (c_lo, n_lo, s_lo, c_lo))
            for ref, (aa, ab, ba, bb) in zip((hi, lo), quads):
                ref[index, pl.ds(start, chunk), 0:width] = aa
                ref[index, pl.ds(start, chunk), width:] = ab
                ref[index, pl.ds(rows + start, chunk), 0:width] = ba
                ref[index, pl.ds(rows + start, chunk), width:] = bb
            return carry

        lax.fori_loop(0, rows // chunk, strip, 0)

    def tables(hi, lo, flip):
        def body(index, carry):
            table(index, hi, lo, flip)
            return carry

        lax.fori_loop(0, lanes, body, 0)

    def remote(src, dst, send, recv, device):
        return pltpu.make_async_remote_copy(
            src_ref=src,
            dst_ref=dst,
            send_sem=send,
            recv_sem=recv,
            device_id=device,
            device_id_type=MESH,
        )

    def volume_copies():
        whole = {"depth": other}
        found = [
            remote(base.at[core], base.at[core], base_sem.at[0], base_sem.at[1], whole),
            remote(
                slowness.at[0],
                slow.at[core, pl.ds(0, rows), :],
                vol_send.at[0],
                vol_recv.at[0],
                whole,
            ),
            remote(
                coef.at[:, 0],
                coefs.at[core, :, pl.ds(halo, rows), :],
                vol_send.at[1],
                vol_recv.at[1],
                whole,
            ),
        ]
        targets = ((core, up, 0), (other, up, 0), (core, down, 1), (other, down, 1))
        for at, (section, place, side) in enumerate(targets):
            found.append(
                remote(
                    parcel.at[side],
                    parcel_in.at[core, side],
                    vol_send.at[2 + at],
                    vol_recv.at[2 + at],
                    {"depth": section, "lat": place},
                )
            )
        return found

    def parcel_rows():
        at = 0
        for stencil in range(stencils - 1):
            size = stencils - 1 - stencil
            yield stencil, at, size
            at += size
        yield stencils, at, stencils

    def pack_parcels():
        for which, at, size in parcel_rows():
            if which < stencils:
                first = coefs[core, which, halo : halo + size, :]
                last = coefs[core, which, halo + rows - size : halo + rows, :]
            else:
                first = slow[core, 0:size, :]
                last = slow[core, rows - size : rows, :]
            parcel[0, at : at + size, :] = first
            parcel[1, at : at + size, :] = last

    def unpack_parcels():
        for level in range(levels):
            for which, at, size in parcel_rows():
                below = parcel_in[level, 0, at : at + size, :]
                above = parcel_in[level, 1, at : at + size, :]
                if which < stencils:
                    coefs[level, which, halo - size : halo, :] = above * inside_first
                    coefs[level, which, halo + rows : halo + rows + size, :] = (
                        below * inside_last
                    )
                else:
                    slow[level, rows : rows + size, :] = above
                    slow[level, rows + size : rows + 2 * size, :] = below

    inside_first = jnp.where(me > 0, 1.0, 0.0)
    inside_last = jnp.where(me < lanes - 1, 1.0, 0.0)

    def wavenumber(index):
        signed = jnp.where(index < count // 2, index, index - count)
        return 2.0 * math.pi / count * signed.astype(jnp.float32)

    def make_phase(level):
        edge_q = (omega * base[level][0:1, :]) ** 2

        def body(index, carry):
            def strip(at, inner):
                start = pl.multiple_of(at * chunk, chunk)
                row = start + lax.broadcasted_iota(jnp.int32, (chunk, width), 0)
                col = lax.broadcasted_iota(jnp.int32, (chunk, width), 1)
                lateral = (
                    wavenumber(row * lanes + index) ** 2 + wavenumber(col * lanes + me) ** 2
                )
                vertical = edge_q - lateral
                root = jnp.sqrt(jnp.abs(vertical))
                sine, cosine = sincos(depth_spacing * root)
                fade = jnp.exp(-depth_spacing * root)
                scale = 1.0 / (count * count)
                moving = vertical > 0
                phase[index, pl.ds(start, chunk), :] = jnp.where(moving, cosine, fade) * scale
                phase[index, pl.ds(rows + start, chunk), :] = (
                    jnp.where(moving, sine, 0.0) * scale
                )
                return inner

            lax.fori_loop(0, rows // chunk, strip, 0)
            return carry

        lax.fori_loop(0, lanes, body, 0)

    quarter = lax.div(me * 4, lanes)
    outer = 1 - lax.div(lax.rem(quarter + 1, 4), 2)

    def peer_at(step):
        place = lax.rem(step + outer * half, lanes - 1)
        beside = lax.div(place, half)
        return far + beside * (near - far) + lax.rem(me + place + beside, half)

    def each_peer(body, low=0, high=lanes - 1):
        def at(step, carry):
            body(peer_at(step))
            return carry

        lax.fori_loop(low, high, at, 0)

    gated = min(gate_step, lanes - 2)

    def take_turn(phase):
        if phase == 2 * levels - 1:
            return

        @pl.when((core == 1) | (phase > 0))
        def _():
            pl.semaphore_wait(turn.at[2 * phase + core], 1)

    def pass_turn(phase, sent_to):
        def one(peer):
            sent_to(peer).wait_send()

        each_peer(one, 0, gated + 1)

        if phase == 2 * levels - 1:
            return

        @pl.when((core == 0) | (phase < 2 * levels - 2))
        def _():
            pl.semaphore_signal(
                turn.at[2 * phase + core + 1],
                inc=1,
                device_id={"depth": other},
                device_id_type=MESH,
            )

    volume = volume_copies()
    swap = remote(
        image.at[other], image_in, image_sem.at[0], image_sem.at[1], {"depth": other}
    )
    for level in range(levels):
        source = 0 if level == 0 else stencils % 2

        if level == 0:

            @pl.when(core == 0)
            def _():
                table(peer_at(0), fwd_hi, fwd_lo, False)

            load.wait()

        def split_rows(at, carry):
            start = pl.multiple_of(at * chunk, chunk)
            values = [
                tuple(
                    field[source, part, pl.ds(own + start, chunk), a * width : (a + 1) * width]
                    for part in range(2)
                )
                for a in range(lanes)
            ]
            for d, (real, imag) in enumerate(short_dft(values, -1)):
                wide[d, pl.ds(start, chunk), 0:width] = real
                wide[d, pl.ds(start, chunk), width:] = imag
            return carry

        lax.fori_loop(0, rows // chunk, split_rows, 0)

        def forward(d):
            hi, lo = split(wide[d, 0:rows, :])
            made = mul(jnp.concatenate([hi, lo], axis=0), fwd_hi[d])
            return made[:rows] + made[rows:] + mul(hi, fwd_lo[d])

        if level == 0:
            pl.semaphore_wait(barrier, lanes + 2)

        def there(peer):
            return remote(
                sent.at[level, peer],
                got.at[level, me],
                send_sem.at[level, 0, peer],
                recv_sem.at[level, 0, me],
                {"lat": peer},
            )

        def send_forward(peer):
            made = forward(peer)
            sent[level, peer, 0:rows, :] = made[:, 0:width]
            sent[level, peer, rows:, :] = made[:, width:]
            there(peer).start()

        def prepare():
            tables(bwd_hi, bwd_lo, True)
            volume[0].wait()
            make_phase(level)

        if level == 0:
            for copy in volume[:3]:
                copy.start()

            @pl.when(core == 1)
            def _():
                prepare()

        if level == 0:

            @pl.when(core == 1)
            def _():
                tables(fwd_hi, fwd_lo, False)

        take_turn(2 * level)
        if level == 0:

            @pl.when(core == 0)
            def _():
                send_forward(peer_at(0))

                def with_table(peer):
                    table(peer, fwd_hi, fwd_lo, False)
                    send_forward(peer)

                each_peer(with_table, 1)
                table(me, fwd_hi, fwd_lo, False)

            @pl.when(core == 1)
            def _():
                each_peer(send_forward)

        else:
            each_peer(send_forward)
        made = forward(me)
        got[level, me, 0:rows, :] = made[:, 0:width]
        got[level, me, rows:, :] = made[:, width:]

        if level == 0:
            for copy in mine:
                copy.wait()
            pack_parcels()
            for copy in volume[3:]:
                copy.start()

            @pl.when(core == 0)
            def _():
                prepare()

        pass_turn(2 * level, there)

        def arrive_forward(peer):
            remote(
                sent.at[level, me],
                got.at[level, peer],
                send_sem.at[level, 0, me],
                recv_sem.at[level, 0, peer],
                {"lat": peer},
            ).wait_recv()

        each_peer(arrive_forward)

        def split_columns(at, carry):
            start = pl.multiple_of(at * chunk, chunk)
            values = [
                (
                    got[level, r, pl.ds(start, chunk), :],
                    got[level, r, pl.ds(rows + start, chunk), :],
                )
                for r in range(lanes)
            ]
            for e, (real, imag) in enumerate(short_dft(values, -1)):
                short[e, pl.ds(start, chunk), :] = real
                short[e, pl.ds(rows + start, chunk), :] = imag
            return carry

        lax.fori_loop(0, rows // chunk, split_columns, 0)

        def left(hi_table, lo_table, values):
            hi, lo = split(values)
            made = mul(hi_table, jnp.concatenate([hi, lo], axis=1))
            return made[:, 0:width] + made[:, width:] + mul(lo_table, hi)

        def column(e, carry):
            after[e] = left(bwd_hi[e], bwd_lo[e], short[e])
            return carry

        def shifted(e, carry):
            real, imag = after[e, 0:rows, :], after[e, rows:, :]
            shift_real, shift_imag = phase[e, 0:rows, :], phase[e, rows:, :]
            moved = jnp.concatenate(
                [
                    real * shift_real - imag * shift_imag,
                    real * shift_imag + imag * shift_real,
                ],
                axis=0,
            )
            after[e] = left(fwd_hi[e], fwd_lo[e], moved)
            return carry

        lax.fori_loop(0, lanes, column, 0, unroll=2)
        lax.fori_loop(0, lanes, shifted, 0, unroll=2)

        def join_columns(at, carry):
            start = pl.multiple_of(at * chunk, chunk)
            values = [
                (after[e, pl.ds(start, chunk), :], after[e, pl.ds(rows + start, chunk), :])
                for e in range(lanes)
            ]
            for r, (real, imag) in enumerate(short_dft(values, 1)):
                back[level, r, 0, pl.ds(start, chunk), :] = real
                back[level, r, 1, pl.ds(start, chunk), :] = imag
            return carry

        lax.fori_loop(0, rows // chunk, join_columns, 0)
        for r in range(lanes):
            for part in range(2):
                back[level, r, part, rows : rows + stencils, :] = back[
                    level, (r - 1) % lanes, part, rows - stencils : rows, :
                ]
                back[level, r, part, rows + stencils : rows + 2 * stencils, :] = back[
                    level, (r + 1) % lanes, part, 0:stencils, :
                ]

        def home(peer):
            return remote(
                back.at[level, peer],
                ret.at[level, me, :, pl.ds(0, wire), :],
                send_sem.at[level, 1, peer],
                recv_sem.at[level, 1, me],
                {"lat": peer},
            )

        take_turn(2 * level + 1)
        each_peer(lambda peer: home(peer).start())

        def inverse(d, real, imag):
            hi, lo = split(jnp.concatenate([real, imag], axis=1))
            wide[d] = mul(hi, bwd_hi[d]) + mul(lo, bwd_hi[d]) + mul(hi, bwd_lo[d])

        for part in range(2):
            ret[level, me, part, 0:wire, :] = back[level, me, part]
        inverse(me, ret[level, me, 0], ret[level, me, 1])
        pass_turn(2 * level + 1, home)

        if level == 0:
            for copy in volume[1:]:
                copy.wait()
            unpack_parcels()

        def make_screen(at, carry):
            start = pl.multiple_of(at * chunk, chunk)
            for a in range(lanes):
                cols = slice(a * width, (a + 1) * width)
                gap = slow[level, pl.ds(start, chunk), cols] - base[level][0:1, :]
                sine, cosine = sincos(depth_spacing * omega * gap)
                screen[0, pl.ds(start, chunk), cols] = cosine
                screen[1, pl.ds(start, chunk), cols] = sine
            return carry

        lax.fori_loop(0, rows // chunk + 1, make_screen, 0)
        if level + 1 < levels:
            make_phase(level + 1)

        def arrive_back(peer):
            remote(
                back.at[level, me],
                ret.at[level, peer, :, pl.ds(0, wire), :],
                send_sem.at[level, 1, me],
                recv_sem.at[level, 1, peer],
                {"lat": peer},
            ).wait_recv()
            inverse(peer, ret[level, peer, 0], ret[level, peer, 1])

        each_peer(arrive_back)

        def screened(start, size):
            values = [
                (wide[d, pl.ds(start, size), 0:width], wide[d, pl.ds(start, size), width:])
                for d in range(lanes)
            ]
            for a, (real, imag) in enumerate(short_dft(values, 1)):
                cols = slice(a * width, (a + 1) * width)
                cosine = screen[0, pl.ds(start, size), cols]
                sine = screen[1, pl.ds(start, size), cols]
                yield cols, (real * cosine - imag * sine, real * sine + imag * cosine)

        def join_rows(at, carry):
            start = pl.multiple_of(at * chunk, chunk)
            for cols, pair in screened(start, chunk):
                for part, value in enumerate(pair):
                    field[0, part, pl.ds(own + start, chunk), cols] = value
            return carry

        lax.fori_loop(0, rows // chunk, join_rows, 0)
        for cols, pair in screened(rows, tile_rows):
            for part, value in enumerate(pair):
                field[0, part, own - stencils : own, cols] = value[0:stencils] * inside_first
                field[0, part, own + rows : own + rows + stencils, cols] = (
                    value[stencils : 2 * stencils] * inside_last
                )

        lane = lax.broadcasted_iota(jnp.int32, (chunk, wide_y), 1)

        def neighbours(ref_at, part, start, center):
            left_one = jnp.where(lane == 0, 0.0, pltpu.roll(center, 1, axis=1))
            right_one = jnp.where(
                lane == wide_y - 1, 0.0, pltpu.roll(center, wide_y - 1, axis=1)
            )
            return (
                field[ref_at, part, start - 1 : start - 1 + chunk, :]
                + field[ref_at, part, start + 1 : start + 1 + chunk, :]
                + left_one
                + right_one
                - 4.0 * center
            )

        for stencil in range(stencils):
            now, later = stencil % 2, (stencil + 1) % 2
            final = stencil == stencils - 1
            for start in range(own if final else top, own + rows if final else top + ext, chunk):
                real = field[now, 0, start : start + chunk, :]
                imag = field[now, 1, start : start + chunk, :]
                weight = coefs[level, stencil, start - top : start - top + chunk, :]
                new_real = real - weight * neighbours(now, 1, start, imag)
                field[later, 0, start : start + chunk, :] = new_real
                if final:
                    image[level, start - own : start - own + chunk, :] = new_real
                field[later, 1, start : start + chunk, :] = imag + weight * neighbours(
                    now, 0, start, real
                )

        @pl.when(core != level)
        def _():
            swap.start()

    def drain(peer):
        for level in range(levels):
            for way, src, dst in (
                (0, sent.at[level, peer], got.at[level, me]),
                (1, back.at[level, peer], ret.at[level, me, :, pl.ds(0, wire), :]),
            ):
                remote(
                    src,
                    dst,
                    send_sem.at[level, way, peer],
                    recv_sem.at[level, way, me],
                    {"lat": peer},
                ).wait_send()

    each_peer(drain, gated + 1)
    swap.wait()
    out[0] = image[core] + image_in[...]


def fused(
    surface, slowness, stencil_coef, base_slowness, base_index, frequency_table, slot_frequency
):
    lanes = lax.axis_size("lat")
    sections = lax.axis_size("depth")
    rows, wide_y = surface.shape[2:]
    stencils = stencil_coef.shape[0]
    width = wide_y // lanes
    halo = -(-stencils // tile_rows) * tile_rows
    ext = rows + 2 * halo
    levels = sections
    parcel = -(-stencils * (stencils + 1) // (2 * tile_rows)) * tile_rows
    f32, bf16 = jnp.float32, jnp.bfloat16
    vmem, smem = pltpu.VMEM, pltpu.SMEM
    sem = pltpu.SemaphoreType.DMA
    anywhere = pl.BlockSpec(memory_space=pltpu.HBM)
    scalar = pl.BlockSpec(memory_space=smem)
    return pl.pallas_call(
        migrate_kernel,
        out_shape=vmem((1, rows, wide_y), f32),
        in_specs=[anywhere] * 3 + [scalar] * 4,
        out_specs=pl.BlockSpec(memory_space=vmem),
        scratch_shapes=[
            vmem((2, 2, ext + 2 * tile_rows, wide_y), f32),
            vmem((lanes, 2 * rows, 2 * width), bf16),
            vmem((lanes, 2 * rows, 2 * width), bf16),
            vmem((lanes, 2 * rows, 2 * width), bf16),
            vmem((lanes, 2 * rows, 2 * width), bf16),
            vmem((lanes, 2 * rows, width), f32),
            vmem((lanes, 2 * rows, width), f32),
            vmem((lanes, 2 * rows, width), f32),
            vmem((levels, lanes, 2 * rows, width), f32),
            vmem((levels, lanes, 2 * rows, width), f32),
            vmem((levels, lanes, 2, rows + tile_rows, width), f32),
            vmem((levels, lanes, 2, rows + chunk, width), f32),
            vmem((lanes, rows + chunk, 2 * width), f32),
            vmem((levels, stencils, ext, wide_y), f32),
            vmem((levels, rows + chunk, wide_y), f32),
            vmem((2, parcel, wide_y), f32),
            vmem((levels, 2, parcel, wide_y), f32),
            vmem((levels, tile_rows, tile_lanes), f32),
            vmem((levels, rows, wide_y), f32),
            vmem((rows, wide_y), f32),
            sem((3,)),
            sem((6,)),
            sem((6,)),
            sem((2,)),
            sem((levels, 2, lanes)),
            sem((levels, 2, lanes)),
            sem((2,)),
            pltpu.SemaphoreType.REGULAR((4 * levels,)),
            vmem((2, rows + chunk, wide_y), f32),
        ],
        compiler_params=pltpu.CompilerParams(
            collective_id=0, has_side_effects=True, vmem_limit_bytes=62 * 2**20
        ),
    )(surface, slowness, stencil_coef, base_slowness, base_index, frequency_table, slot_frequency)


def migrate(*arrays):
    surface, slowness, stencil_coef = arrays[:3]
    lanes = lax.axis_size("lat")
    sections = lax.axis_size("depth")
    rows, wide_y = surface.shape[2:]
    fits = (
        rows * lanes == wide_y
        and rows == tile_lanes
        and lanes > 1
        and lanes & (lanes - 1) == 0
        and sections == 2
        and surface.shape[0] == sections
        and slowness.shape[0] == 1
        and 0 < 2 * stencil_coef.shape[0] <= tile_rows
    )
    return fused(*arrays) if fits else shards(*arrays)


def solution(mesh):
    placed = (
        P("shots", None, "lat", None),
        P("depth", "lat", None),
        P(None, "depth", "lat", None),
        P(),
        P("depth"),
        P(),
        P("shots"),
    )
    return jax.shard_map(
        migrate,
        mesh=mesh,
        in_specs=placed,
        out_specs=P(("shots", "depth"), "lat", None),
        check_vma=False,
    )
```

```python
import math

import jax
import jax.numpy as jnp
from jax import lax
from jax.experimental import pallas as pl
from jax.experimental.pallas import tpu as pltpu
from jax.sharding import PartitionSpec as P

depth_spacing = 1.0
highest = lax.Precision.HIGHEST


def with_halo(cells, sides, width):
    for axis, dim in sides:
        count = lax.axis_size(axis)
        ends = count - 1
        head = lax.slice_in_dim(cells, 0, width, axis=dim)
        tail = lax.slice_in_dim(cells, cells.shape[dim] - width, cells.shape[dim], axis=dim)
        cells = jnp.concatenate(
            [
                lax.ppermute(tail, axis, [(i, (i + 1) % count) for i in range(ends)]),
                cells,
                lax.ppermute(head, axis, [((i + 1) % count, i) for i in range(ends)]),
            ],
            axis=dim,
        )
    return cells


def dft_table(count):
    row_index = lax.broadcasted_iota(jnp.int32, (count, count), 0)
    col_index = lax.broadcasted_iota(jnp.int32, (count, count), 1)
    angle = 2.0 * math.pi / count * (row_index * col_index % count).astype(jnp.float32)
    return (jnp.cos(angle), jnp.sin(angle))


def wavenumbers(index, count):
    signed = jnp.where(index < count // 2, index, index - count)
    return 2.0 * math.pi / count * signed.astype(jnp.float32)


def along_last(values, table):
    return jnp.einsum("brn,nk->brk", values, table, precision=highest)


def along_middle(values, table):
    return jnp.einsum("bxk,xj->bkj", values, table, precision=highest)


def pair_last(pair, table):
    batch = pair.shape[0]
    merged = pair.reshape((batch * 2,) + pair.shape[2:])
    result = along_last(merged, table)
    return result.reshape((batch, 2) + result.shape[1:])


def pair_middle(pair, table):
    batch = pair.shape[0]
    merged = pair.reshape((batch * 2,) + pair.shape[2:])
    result = along_middle(merged, table)
    return result.reshape((batch, 2) + result.shape[1:])


def stencil_sum(extended):
    center = extended[:, :, 1:-1]
    sideways = jnp.pad(center, ((0, 0), (0, 0), (0, 0), (1, 1)))
    return (
        extended[:, :, 2:]
        + extended[:, :, :-2]
        + sideways[..., 2:]
        + sideways[..., :-2]
        - 4.0 * center
    )


def correct(wavefield, stencil_value, coefficient):
    real_part = wavefield[:, 0] - coefficient[None] * stencil_value[:, 1]
    imag_part = wavefield[:, 1] + coefficient[None] * stencil_value[:, 0]
    return jnp.stack((real_part, imag_part), axis=1)


def shards(
    surface, slowness, stencil_coef, base_slowness, base_index, frequency_table, slot_frequency
):
    section_index = lax.axis_index("depth")
    sections = lax.axis_size("depth")
    lanes = lax.axis_size("lat")
    slots = surface.shape[0]
    rows = surface.shape[2]
    width_y = surface.shape[3]
    width_x = rows * lanes
    block_y = width_y // lanes
    steps_here = slowness.shape[0]
    stencils = stencil_coef.shape[0]
    cos_x, sin_x = dft_table(width_x)
    cos_y, sin_y = dft_table(width_y)
    wave_x = wavenumbers(lax.broadcasted_iota(jnp.int32, (width_x,), 0), width_x)[None, None, :]
    local_y = lax.axis_index("lat") * block_y + lax.broadcasted_iota(jnp.int32, (block_y,), 0)
    wave_y = wavenumbers(local_y, width_y)[None, :, None]
    lateral = wave_x**2 + wave_y**2
    table_freq = lax.broadcasted_iota(jnp.int32, (1, frequency_table.shape[0]), 1)
    omegas = jnp.sum(
        jnp.where(slot_frequency[:, None] == table_freq, frequency_table[None, :], 0.0), axis=1
    )
    table_base = lax.broadcasted_iota(jnp.int32, (1, base_slowness.shape[0]), 1)
    base_values = jnp.sum(
        jnp.where(base_index[:, None] == table_base, base_slowness[None, :], 0.0), axis=1
    )
    volume_slow, volume_coef, volume_base = (
        lax.all_gather(slowness, "depth", axis=0, tiled=True),
        lax.all_gather(stencil_coef, "depth", axis=1, tiled=True),
        lax.all_gather(base_values, "depth", axis=0, tiled=True),
    )
    levels = steps_here * sections
    mine = slots // sections
    first_mine = section_index * mine
    wavefield = lax.dynamic_slice_in_dim(surface, first_mine, mine, 0)
    freqs = lax.dynamic_slice_in_dim(omegas, first_mine, mine, 0)
    partial_layers = []
    for level in range(levels):
        depth_wavefield = wavefield
        batch = depth_wavefield.shape[0]
        base_value = volume_base[level]
        with_cos = pair_last(depth_wavefield, cos_y)
        with_sin = pair_last(depth_wavefield, sin_y)
        fwd_real = with_cos[:, 0] + with_sin[:, 1]
        fwd_imag = with_cos[:, 1] - with_sin[:, 0]
        packed = jnp.stack((fwd_real, fwd_imag), axis=1).reshape(batch, 2, rows, lanes, block_y)
        columns = lax.all_to_all(packed, "lat", split_axis=3, concat_axis=2, tiled=True).reshape(
            batch, 2, width_x, block_y
        )
        col_cos = pair_middle(columns, cos_x)
        col_sin = pair_middle(columns, sin_x)
        spec_real = col_cos[:, 0] + col_sin[:, 1]
        spec_imag = col_cos[:, 1] - col_sin[:, 0]
        vertical = ((freqs * base_value) ** 2)[:, None, None] - lateral
        root = jnp.sqrt(jnp.abs(vertical))
        shift_real = jnp.where(
            vertical > 0, jnp.cos(depth_spacing * root), jnp.exp(-depth_spacing * root)
        )
        shift_imag = jnp.where(vertical > 0, jnp.sin(depth_spacing * root), 0.0)
        moved = jnp.stack(
            (
                spec_real * shift_real - spec_imag * shift_imag,
                spec_real * shift_imag + spec_imag * shift_real,
            ),
            axis=1,
        )
        back_cos = pair_last(moved, cos_x)
        back_sin = pair_last(moved, sin_x)
        back_real = back_cos[:, 0] - back_sin[:, 1]
        back_imag = back_cos[:, 1] + back_sin[:, 0]
        packed = jnp.stack((back_real, back_imag), axis=1).reshape(batch, 2, block_y, lanes, rows)
        returned = lax.all_to_all(packed, "lat", split_axis=3, concat_axis=2, tiled=True).reshape(
            batch, 2, width_y, rows
        )
        scale = 1.0 / (width_x * width_y)
        ret_cos = pair_middle(returned, cos_y)
        ret_sin = pair_middle(returned, sin_y)
        out_real = (ret_cos[:, 0] - ret_sin[:, 1]) * scale
        out_imag = (ret_cos[:, 1] + ret_sin[:, 0]) * scale
        screen = depth_spacing * freqs[:, None, None] * (volume_slow[level] - base_value)[None]
        cosine = jnp.cos(screen)
        sine = jnp.sin(screen)
        depth_wavefield = jnp.stack(
            (out_real * cosine - out_imag * sine, out_real * sine + out_imag * cosine), axis=1
        )
        for stencil in range(stencils):
            extended = with_halo(depth_wavefield, (("lat", 2),), 1)
            depth_wavefield = correct(
                depth_wavefield, stencil_sum(extended), volume_coef[stencil, level]
            )
        wavefield = depth_wavefield
        partial_layers.append(jnp.sum(wavefield[:, 0], axis=0))
    partial_image = jnp.stack(partial_layers)
    return lax.psum_scatter(partial_image, "depth", scatter_dimension=0, tiled=True)


MESH = pl.DeviceIdType.MESH
tile_rows = 8
tile_lanes = 128
chunk = 16
gate_step = 2


def times_root(value, power, count, sign):
    real, imag = value
    turn = (power * 8 // count) % 8 if (power * 8) % count == 0 else None
    half = math.sqrt(0.5)
    if turn == 0:
        return value
    if turn == 2:
        return (-imag, real) if sign > 0 else (imag, -real)
    if turn == 1:
        if sign > 0:
            return ((real - imag) * half, (real + imag) * half)
        return ((real + imag) * half, (imag - real) * half)
    if turn == 3:
        if sign > 0:
            return (-(real + imag) * half, (real - imag) * half)
        return ((imag - real) * half, -(real + imag) * half)
    angle = sign * 2.0 * math.pi * power / count
    cosine, sine = math.cos(angle), math.sin(angle)
    return (real * cosine - imag * sine, real * sine + imag * cosine)


def short_dft(values, sign):
    count = len(values)
    if count == 1:
        return values
    even = short_dft(values[0::2], sign)
    odd = short_dft(values[1::2], sign)
    low, high = [], []
    for power in range(count // 2):
        turned = times_root(odd[power], power, count, sign)
        low.append((even[power][0] + turned[0], even[power][1] + turned[1]))
        high.append((even[power][0] - turned[0], even[power][1] - turned[1]))
    return low + high


def quarter_sincos(rest, quarter):
    square = rest * rest
    sine = rest + rest * square * (
        -1.6666654611e-1 + square * (8.3321608736e-3 + square * -1.9515295891e-4)
    )
    cosine = (
        1.0
        - 0.5 * square
        + square
        * square
        * (4.166664568298827e-2 + square * (-1.388731625493765e-3 + square * 2.443315711809948e-5))
    )
    swap = quarter % 2 == 1
    first = jnp.where(swap, cosine, sine)
    second = jnp.where(swap, sine, cosine)
    turn = quarter % 4
    return (
        jnp.where(turn >= 2, -first, first),
        jnp.where((turn == 1) | (turn == 2), -second, second),
    )


def sincos(angle):
    nearest = jnp.floor(angle * (2.0 / math.pi) + 0.5)
    rest = angle - nearest * 1.5703125
    rest = rest - nearest * 4.83751296997e-4
    rest = rest - nearest * 7.54978995489e-8
    return quarter_sincos(rest, nearest.astype(jnp.int32) & 3)


def split(values):
    high = values.astype(jnp.bfloat16)
    return high, (values - high.astype(jnp.float32)).astype(jnp.bfloat16)


def mul(left, right):
    return jnp.dot(left, right, preferred_element_type=jnp.float32)


def migrate_kernel(
    surface,
    slowness,
    coef,
    base_table,
    base_index,
    freq_table,
    slot_freq,
    out,
    field,
    fwd_hi,
    fwd_lo,
    bwd_hi,
    bwd_lo,
    short,
    after,
    phase,
    sent,
    got,
    back,
    ret,
    wide,
    coefs,
    slow,
    parcel,
    parcel_in,
    base,
    image,
    image_in,
    load_sem,
    vol_send,
    vol_recv,
    base_sem,
    send_sem,
    recv_sem,
    image_sem,
    turn,
    screen,
):
    lanes, rows2, width = short.shape
    rows = rows2 // 2
    ext = coefs.shape[2]
    halo = (ext - rows) // 2
    count = lanes * rows
    levels = coefs.shape[0]
    wire = rows + tile_rows
    half = lanes // 2
    far = lax.rem(lax.div(lax.axis_index("lat"), half) + 1, 2) * half
    near = lax.div(lax.axis_index("lat"), half) * half
    stencils = coef.shape[0]
    top = tile_rows
    own = top + halo
    me = lax.axis_index("lat")
    core = lax.axis_index("depth")
    other = 1 - core
    up = lax.rem(me + lanes - 1, lanes)
    down = lax.rem(me + 1, lanes)

    barrier = pltpu.get_barrier_semaphore()
    for step in range(1, lanes):
        pl.semaphore_signal(
            barrier,
            inc=1,
            device_id={"lat": lax.rem(me + step, lanes)},
            device_id_type=MESH,
        )
    for place in (me, up, down):
        pl.semaphore_signal(
            barrier, inc=1, device_id={"depth": other, "lat": place}, device_id_type=MESH
        )

    load = pltpu.make_async_copy(
        surface.at[core], field.at[0, :, pl.ds(own, rows), :], load_sem.at[0]
    )
    load.start()
    mine = [
        pltpu.make_async_copy(
            slowness.at[0], slow.at[core, pl.ds(0, rows), :], load_sem.at[1]
        ),
        pltpu.make_async_copy(
            coef.at[:, 0], coefs.at[core, :, pl.ds(halo, rows), :], load_sem.at[2]
        ),
    ]
    for copy in mine:
        copy.start()

    omega = freq_table[slot_freq[core]]
    base[core] = jnp.full(base.shape[1:], base_table[base_index[0]], jnp.float32)
    wide_y = field.shape[3]
    back[:, :, :, rows:, :] = jnp.zeros((levels, lanes, 2, tile_rows, width), jnp.float32)
    ret[:, :, :, rows:, :] = jnp.zeros((levels, lanes, 2, chunk, width), jnp.float32)
    slow[:, rows:, :] = jnp.zeros((levels, chunk, wide_y), jnp.float32)
    parcel[...] = jnp.zeros(parcel.shape, jnp.float32)
    rim = jnp.zeros((levels, stencils, halo, wide_y), jnp.float32)
    coefs[:, :, 0:halo, :] = rim
    coefs[:, :, halo + rows :, :] = rim
    edge = jnp.zeros((2, 2, top + halo, wide_y), jnp.float32)
    field[:, :, 0:own, :] = edge
    field[:, :, own + rows :, :] = edge

    def table(index, hi, lo, flip):
        def strip(at, carry):
            start = pl.multiple_of(at * chunk, chunk)
            row = start + lax.broadcasted_iota(jnp.int32, (chunk, width), 0)
            col = lax.broadcasted_iota(jnp.int32, (chunk, width), 1)
            power = col * (row * lanes + index) if flip else row * (col * lanes + index)
            power = power & (count - 1)
            quarter = (4 * power + count // 2) // count
            rest = power - quarter * (count // 4)
            sine, cosine = quarter_sincos(
                rest.astype(jnp.float32) * (2.0 * math.pi / count), quarter & 3
            )
            c_hi, c_lo = split(cosine)
            s_hi, s_lo = split(sine)
            n_hi, n_lo = -s_hi, -s_lo
            if flip:
                quads = ((c_hi, s_hi, n_hi, c_hi), (c_lo, s_lo, n_lo, c_lo))
            else:
                quads = ((c_hi, n_hi, s_hi, c_hi), (c_lo, n_lo, s_lo, c_lo))
            for ref, (aa, ab, ba, bb) in zip((hi, lo), quads):
                ref[index, pl.ds(start, chunk), 0:width] = aa
                ref[index, pl.ds(start, chunk), width:] = ab
                ref[index, pl.ds(rows + start, chunk), 0:width] = ba
                ref[index, pl.ds(rows + start, chunk), width:] = bb
            return carry

        lax.fori_loop(0, rows // chunk, strip, 0)

    def tables(hi, lo, flip):
        def body(index, carry):
            table(index, hi, lo, flip)
            return carry

        lax.fori_loop(0, lanes, body, 0)

    def remote(src, dst, send, recv, device):
        return pltpu.make_async_remote_copy(
            src_ref=src,
            dst_ref=dst,
            send_sem=send,
            recv_sem=recv,
            device_id=device,
            device_id_type=MESH,
        )

    def volume_copies():
        whole = {"depth": other}
        found = [
            remote(base.at[core], base.at[core], base_sem.at[0], base_sem.at[1], whole),
            remote(
                slowness.at[0],
                slow.at[core, pl.ds(0, rows), :],
                vol_send.at[0],
                vol_recv.at[0],
                whole,
            ),
            remote(
                coef.at[:, 0],
                coefs.at[core, :, pl.ds(halo, rows), :],
                vol_send.at[1],
                vol_recv.at[1],
                whole,
            ),
        ]
        targets = ((core, up, 0), (other, up, 0), (core, down, 1), (other, down, 1))
        for at, (section, place, side) in enumerate(targets):
            found.append(
                remote(
                    parcel.at[side],
                    parcel_in.at[core, side],
                    vol_send.at[2 + at],
                    vol_recv.at[2 + at],
                    {"depth": section, "lat": place},
                )
            )
        return found

    def parcel_rows():
        at = 0
        for stencil in range(stencils - 1):
            size = stencils - 1 - stencil
            yield stencil, at, size
            at += size
        yield stencils, at, stencils

    def pack_parcels():
        for which, at, size in parcel_rows():
            if which < stencils:
                first = coefs[core, which, halo : halo + size, :]
                last = coefs[core, which, halo + rows - size : halo + rows, :]
            else:
                first = slow[core, 0:size, :]
                last = slow[core, rows - size : rows, :]
            parcel[0, at : at + size, :] = first
            parcel[1, at : at + size, :] = last

    def unpack_parcels():
        for level in range(levels):
            for which, at, size in parcel_rows():
                below = parcel_in[level, 0, at : at + size, :]
                above = parcel_in[level, 1, at : at + size, :]
                if which < stencils:
                    coefs[level, which, halo - size : halo, :] = above * inside_first
                    coefs[level, which, halo + rows : halo + rows + size, :] = (
                        below * inside_last
                    )
                else:
                    slow[level, rows : rows + size, :] = above
                    slow[level, rows + size : rows + 2 * size, :] = below

    inside_first = jnp.where(me > 0, 1.0, 0.0)
    inside_last = jnp.where(me < lanes - 1, 1.0, 0.0)

    def wavenumber(index):
        signed = jnp.where(index < count // 2, index, index - count)
        return 2.0 * math.pi / count * signed.astype(jnp.float32)

    def make_phase(level):
        edge_q = (omega * base[level][0:1, :]) ** 2

        def body(index, carry):
            def strip(at, inner):
                start = pl.multiple_of(at * chunk, chunk)
                row = start + lax.broadcasted_iota(jnp.int32, (chunk, width), 0)
                col = lax.broadcasted_iota(jnp.int32, (chunk, width), 1)
                lateral = (
                    wavenumber(row * lanes + index) ** 2 + wavenumber(col * lanes + me) ** 2
                )
                vertical = edge_q - lateral
                root = jnp.sqrt(jnp.abs(vertical))
                sine, cosine = sincos(depth_spacing * root)
                fade = jnp.exp(-depth_spacing * root)
                scale = 1.0 / (count * count)
                moving = vertical > 0
                phase[index, pl.ds(start, chunk), :] = jnp.where(moving, cosine, fade) * scale
                phase[index, pl.ds(rows + start, chunk), :] = (
                    jnp.where(moving, sine, 0.0) * scale
                )
                return inner

            lax.fori_loop(0, rows // chunk, strip, 0)
            return carry

        lax.fori_loop(0, lanes, body, 0)

    quarter = lax.div(me * 4, lanes)
    outer = 1 - lax.div(lax.rem(quarter + 1, 4), 2)

    def peer_at(step):
        place = lax.rem(step + outer * half, lanes - 1)
        beside = lax.div(place, half)
        return far + beside * (near - far) + lax.rem(me + place + beside, half)

    def each_peer(body, low=0, high=lanes - 1):
        def at(step, carry):
            body(peer_at(step))
            return carry

        lax.fori_loop(low, high, at, 0)

    gated = min(gate_step, lanes - 2)

    def take_turn(phase):
        if phase == 2 * levels - 1:
            return

        @pl.when((core == 1) | (phase > 0))
        def _():
            pl.semaphore_wait(turn.at[2 * phase + core], 1)

    def pass_turn(phase, sent_to):
        def one(peer):
            sent_to(peer).wait_send()

        each_peer(one, 0, gated + 1)

        if phase == 2 * levels - 1:
            return

        @pl.when((core == 0) | (phase < 2 * levels - 2))
        def _():
            pl.semaphore_signal(
                turn.at[2 * phase + core + 1],
                inc=1,
                device_id={"depth": other},
                device_id_type=MESH,
            )

    volume = volume_copies()
    swap = remote(
        image.at[other], image_in, image_sem.at[0], image_sem.at[1], {"depth": other}
    )
    for level in range(levels):
        source = 0 if level == 0 else stencils % 2

        if level == 0:

            @pl.when(core == 0)
            def _():
                table(peer_at(0), fwd_hi, fwd_lo, False)

            load.wait()

        def split_rows(at, carry):
            start = pl.multiple_of(at * chunk, chunk)
            values = [
                tuple(
                    field[source, part, pl.ds(own + start, chunk), a * width : (a + 1) * width]
                    for part in range(2)
                )
                for a in range(lanes)
            ]
            for d, (real, imag) in enumerate(short_dft(values, -1)):
                wide[d, pl.ds(start, chunk), 0:width] = real
                wide[d, pl.ds(start, chunk), width:] = imag
            return carry

        lax.fori_loop(0, rows // chunk, split_rows, 0)

        def forward(d):
            hi, lo = split(wide[d, 0:rows, :])
            made = mul(jnp.concatenate([hi, lo], axis=0), fwd_hi[d])
            return made[:rows] + made[rows:] + mul(hi, fwd_lo[d])

        if level == 0:
            pl.semaphore_wait(barrier, lanes + 2)

        def there(peer):
            return remote(
                sent.at[level, peer],
                got.at[level, me],
                send_sem.at[level, 0, peer],
                recv_sem.at[level, 0, me],
                {"lat": peer},
            )

        def send_forward(peer):
            made = forward(peer)
            sent[level, peer, 0:rows, :] = made[:, 0:width]
            sent[level, peer, rows:, :] = made[:, width:]
            there(peer).start()

        def prepare():
            tables(bwd_hi, bwd_lo, True)
            volume[0].wait()
            make_phase(level)

        if level == 0:
            for copy in volume[:3]:
                copy.start()

            @pl.when(core == 1)
            def _():
                prepare()

        if level == 0:

            @pl.when(core == 1)
            def _():
                tables(fwd_hi, fwd_lo, False)

        take_turn(2 * level)
        if level == 0:

            @pl.when(core == 0)
            def _():
                send_forward(peer_at(0))

                def with_table(peer):
                    table(peer, fwd_hi, fwd_lo, False)
                    send_forward(peer)

                each_peer(with_table, 1)
                table(me, fwd_hi, fwd_lo, False)

            @pl.when(core == 1)
            def _():
                each_peer(send_forward)

        else:
            each_peer(send_forward)
        made = forward(me)
        got[level, me, 0:rows, :] = made[:, 0:width]
        got[level, me, rows:, :] = made[:, width:]

        if level == 0:
            for copy in mine:
                copy.wait()
            pack_parcels()
            for copy in volume[3:]:
                copy.start()

            @pl.when(core == 0)
            def _():
                prepare()

        pass_turn(2 * level, there)

        def arrive_forward(peer):
            remote(
                sent.at[level, me],
                got.at[level, peer],
                send_sem.at[level, 0, me],
                recv_sem.at[level, 0, peer],
                {"lat": peer},
            ).wait_recv()

        each_peer(arrive_forward)

        def split_columns(at, carry):
            start = pl.multiple_of(at * chunk, chunk)
            values = [
                (
                    got[level, r, pl.ds(start, chunk), :],
                    got[level, r, pl.ds(rows + start, chunk), :],
                )
                for r in range(lanes)
            ]
            for e, (real, imag) in enumerate(short_dft(values, -1)):
                short[e, pl.ds(start, chunk), :] = real
                short[e, pl.ds(rows + start, chunk), :] = imag
            return carry

        lax.fori_loop(0, rows // chunk, split_columns, 0)

        def left(hi_table, lo_table, values):
            hi, lo = split(values)
            made = mul(hi_table, jnp.concatenate([hi, lo], axis=1))
            return made[:, 0:width] + made[:, width:] + mul(lo_table, hi)

        def column(e, carry):
            after[e] = left(bwd_hi[e], bwd_lo[e], short[e])
            return carry

        def shifted(e, carry):
            real, imag = after[e, 0:rows, :], after[e, rows:, :]
            shift_real, shift_imag = phase[e, 0:rows, :], phase[e, rows:, :]
            moved = jnp.concatenate(
                [
                    real * shift_real - imag * shift_imag,
                    real * shift_imag + imag * shift_real,
                ],
                axis=0,
            )
            after[e] = left(fwd_hi[e], fwd_lo[e], moved)
            return carry

        lax.fori_loop(0, lanes, column, 0, unroll=2)
        lax.fori_loop(0, lanes, shifted, 0, unroll=2)

        def join_columns(at, carry):
            start = pl.multiple_of(at * chunk, chunk)
            values = [
                (after[e, pl.ds(start, chunk), :], after[e, pl.ds(rows + start, chunk), :])
                for e in range(lanes)
            ]
            for r, (real, imag) in enumerate(short_dft(values, 1)):
                back[level, r, 0, pl.ds(start, chunk), :] = real
                back[level, r, 1, pl.ds(start, chunk), :] = imag
            return carry

        lax.fori_loop(0, rows // chunk, join_columns, 0)
        for r in range(lanes):
            for part in range(2):
                back[level, r, part, rows : rows + stencils, :] = back[
                    level, (r - 1) % lanes, part, rows - stencils : rows, :
                ]
                back[level, r, part, rows + stencils : rows + 2 * stencils, :] = back[
                    level, (r + 1) % lanes, part, 0:stencils, :
                ]

        def home(peer):
            return remote(
                back.at[level, peer],
                ret.at[level, me, :, pl.ds(0, wire), :],
                send_sem.at[level, 1, peer],
                recv_sem.at[level, 1, me],
                {"lat": peer},
            )

        take_turn(2 * level + 1)
        each_peer(lambda peer: home(peer).start())

        def inverse(d, real, imag):
            hi, lo = split(jnp.concatenate([real, imag], axis=1))
            wide[d] = mul(hi, bwd_hi[d]) + mul(lo, bwd_hi[d]) + mul(hi, bwd_lo[d])

        for part in range(2):
            ret[level, me, part, 0:wire, :] = back[level, me, part]
        inverse(me, ret[level, me, 0], ret[level, me, 1])
        pass_turn(2 * level + 1, home)

        if level == 0:
            for copy in volume[1:]:
                copy.wait()
            unpack_parcels()

        def make_screen(at, carry):
            start = pl.multiple_of(at * chunk, chunk)
            for a in range(lanes):
                cols = slice(a * width, (a + 1) * width)
                gap = slow[level, pl.ds(start, chunk), cols] - base[level][0:1, :]
                sine, cosine = sincos(depth_spacing * omega * gap)
                screen[0, pl.ds(start, chunk), cols] = cosine
                screen[1, pl.ds(start, chunk), cols] = sine
            return carry

        lax.fori_loop(0, rows // chunk + 1, make_screen, 0)
        if level + 1 < levels:
            make_phase(level + 1)

        def arrive_back(peer):
            remote(
                back.at[level, me],
                ret.at[level, peer, :, pl.ds(0, wire), :],
                send_sem.at[level, 1, me],
                recv_sem.at[level, 1, peer],
                {"lat": peer},
            ).wait_recv()
            inverse(peer, ret[level, peer, 0], ret[level, peer, 1])

        each_peer(arrive_back)

        def screened(start, size):
            values = [
                (wide[d, pl.ds(start, size), 0:width], wide[d, pl.ds(start, size), width:])
                for d in range(lanes)
            ]
            for a, (real, imag) in enumerate(short_dft(values, 1)):
                cols = slice(a * width, (a + 1) * width)
                cosine = screen[0, pl.ds(start, size), cols]
                sine = screen[1, pl.ds(start, size), cols]
                yield cols, (real * cosine - imag * sine, real * sine + imag * cosine)

        def join_rows(at, carry):
            start = pl.multiple_of(at * chunk, chunk)
            for cols, pair in screened(start, chunk):
                for part, value in enumerate(pair):
                    field[0, part, pl.ds(own + start, chunk), cols] = value
            return carry

        lax.fori_loop(0, rows // chunk, join_rows, 0)
        for cols, pair in screened(rows, tile_rows):
            for part, value in enumerate(pair):
                field[0, part, own - stencils : own, cols] = value[0:stencils] * inside_first
                field[0, part, own + rows : own + rows + stencils, cols] = (
                    value[stencils : 2 * stencils] * inside_last
                )

        lane = lax.broadcasted_iota(jnp.int32, (chunk, wide_y), 1)

        def neighbours(ref_at, part, start, center):
            left_one = jnp.where(lane == 0, 0.0, pltpu.roll(center, 1, axis=1))
            right_one = jnp.where(
                lane == wide_y - 1, 0.0, pltpu.roll(center, wide_y - 1, axis=1)
            )
            return (
                field[ref_at, part, start - 1 : start - 1 + chunk, :]
                + field[ref_at, part, start + 1 : start + 1 + chunk, :]
                + left_one
                + right_one
                - 4.0 * center
            )

        for stencil in range(stencils):
            now, later = stencil % 2, (stencil + 1) % 2
            final = stencil == stencils - 1
            for start in range(own if final else top, own + rows if final else top + ext, chunk):
                real = field[now, 0, start : start + chunk, :]
                imag = field[now, 1, start : start + chunk, :]
                weight = coefs[level, stencil, start - top : start - top + chunk, :]
                new_real = real - weight * neighbours(now, 1, start, imag)
                if not final or level < levels - 1:
                    field[later, 0, start : start + chunk, :] = new_real
                if final:
                    image[level, start - own : start - own + chunk, :] = new_real
                if not final or level < levels - 1:
                    field[later, 1, start : start + chunk, :] = imag + weight * neighbours(
                        now, 0, start, real
                    )

        @pl.when(core != level)
        def _():
            swap.start()

    def drain(peer):
        for level in range(levels):
            for way, src, dst in (
                (0, sent.at[level, peer], got.at[level, me]),
                (1, back.at[level, peer], ret.at[level, me, :, pl.ds(0, wire), :]),
            ):
                remote(
                    src,
                    dst,
                    send_sem.at[level, way, peer],
                    recv_sem.at[level, way, me],
                    {"lat": peer},
                ).wait_send()

    each_peer(drain, gated + 1)
    swap.wait()
    out[0] = image[core] + image_in[...]


def fused(
    surface, slowness, stencil_coef, base_slowness, base_index, frequency_table, slot_frequency
):
    lanes = lax.axis_size("lat")
    sections = lax.axis_size("depth")
    rows, wide_y = surface.shape[2:]
    stencils = stencil_coef.shape[0]
    width = wide_y // lanes
    halo = -(-stencils // tile_rows) * tile_rows
    ext = rows + 2 * halo
    levels = sections
    parcel = -(-stencils * (stencils + 1) // (2 * tile_rows)) * tile_rows
    f32, bf16 = jnp.float32, jnp.bfloat16
    vmem, smem = pltpu.VMEM, pltpu.SMEM
    sem = pltpu.SemaphoreType.DMA
    anywhere = pl.BlockSpec(memory_space=pltpu.HBM)
    scalar = pl.BlockSpec(memory_space=smem)
    return pl.pallas_call(
        migrate_kernel,
        out_shape=vmem((1, rows, wide_y), f32),
        in_specs=[anywhere] * 3 + [scalar] * 4,
        out_specs=pl.BlockSpec(memory_space=vmem),
        scratch_shapes=[
            vmem((2, 2, ext + 2 * tile_rows, wide_y), f32),
            vmem((lanes, 2 * rows, 2 * width), bf16),
            vmem((lanes, 2 * rows, 2 * width), bf16),
            vmem((lanes, 2 * rows, 2 * width), bf16),
            vmem((lanes, 2 * rows, 2 * width), bf16),
            vmem((lanes, 2 * rows, width), f32),
            vmem((lanes, 2 * rows, width), f32),
            vmem((lanes, 2 * rows, width), f32),
            vmem((levels, lanes, 2 * rows, width), f32),
            vmem((levels, lanes, 2 * rows, width), f32),
            vmem((levels, lanes, 2, rows + tile_rows, width), f32),
            vmem((levels, lanes, 2, rows + chunk, width), f32),
            vmem((lanes, rows + chunk, 2 * width), f32),
            vmem((levels, stencils, ext, wide_y), f32),
            vmem((levels, rows + chunk, wide_y), f32),
            vmem((2, parcel, wide_y), f32),
            vmem((levels, 2, parcel, wide_y), f32),
            vmem((levels, tile_rows, tile_lanes), f32),
            vmem((levels, rows, wide_y), f32),
            vmem((rows, wide_y), f32),
            sem((3,)),
            sem((6,)),
            sem((6,)),
            sem((2,)),
            sem((levels, 2, lanes)),
            sem((levels, 2, lanes)),
            sem((2,)),
            pltpu.SemaphoreType.REGULAR((4 * levels,)),
            vmem((2, rows + chunk, wide_y), f32),
        ],
        compiler_params=pltpu.CompilerParams(
            collective_id=0, has_side_effects=True, vmem_limit_bytes=62 * 2**20
        ),
    )(surface, slowness, stencil_coef, base_slowness, base_index, frequency_table, slot_frequency)


def migrate(*arrays):
    surface, slowness, stencil_coef = arrays[:3]
    lanes = lax.axis_size("lat")
    sections = lax.axis_size("depth")
    rows, wide_y = surface.shape[2:]
    fits = (
        rows * lanes == wide_y
        and rows == tile_lanes
        and lanes > 1
        and lanes & (lanes - 1) == 0
        and sections == 2
        and surface.shape[0] == sections
        and slowness.shape[0] == 1
        and 0 < 2 * stencil_coef.shape[0] <= tile_rows
    )
    return fused(*arrays) if fits else shards(*arrays)


def solution(mesh):
    placed = (
        P("shots", None, "lat", None),
        P("depth", "lat", None),
        P(None, "depth", "lat", None),
        P(),
        P("depth"),
        P(),
        P("shots"),
    )
    return jax.shard_map(
        migrate,
        mesh=mesh,
        in_specs=placed,
        out_specs=P(("shots", "depth"), "lat", None),
        check_vma=False,
    )
```
